32 devices in a mesh: tile: 8 (over y, x, core), mode: 4 (over z).
Axes of the slice: x: 2, y: 2, z: 4, core: 2. Of those that a mesh axis runs over, the one named last changes fastest.
Arguments:
- object_field: float32 [2, 2, 2048, 384], P(None, None, 'tile'), may hold values from -4 to 4
- probe: float32 [8, 2, 256, 256], P('mode'), may hold values from -4 to 4
- measured: float32 [32, 256, 256], P('tile'), may hold values from 0 to 16
- prop_phase: float32 [256, 256], replicated, may hold values from -3.140625 to 3.140625
- counts: int32 [8], P('tile'), may hold values from 1 to 4, 16 in all
- row_offset: int32 [32], P('tile'), may hold values from 0 to 255
- col_offset: int32 [32], P('tile'), may hold values from 0 to 128
Outputs:
- object_grad: float32 [2, 2, 2048, 384], P(None, None, 'tile')
- probe_grad: float32 [8, 2, 256, 256], P('mode')
The draws below stay inside these ranges and needn't reach their ends.
Inputs may be any that keep to these rules, and one draw needn't show every extreme that they name: Slot i is live for i % 4 < counts[i // 4]; some tile has all 4 slots live.
All inputs are finite; a program needn't handle non-finite values. No bound on the sum of `counts` on one device may be relied on, other than what follows from the above.
Results may differ from the reference program's by a relative error of at most 0.0003.
Values sent between devices are 32-bit elements; how exact they have to be, the bound alone decides.
A program may use at most 128 MiB of HBM per device.

```python
import math
import jax
import jax.numpy as jnp
import numpy as np
from jax import lax

WIN = 256
MODES = 8
SLICES = 2
CAP = 4
TILE_ROWS = 256
COLS = 384
ROWS = 2048
POSITIONS = 32
N_TILE = 8


def with_ends(values, key, least, largest):
    shape = values.shape
    spot = [jax.random.randint(jax.random.fold_in(key, axis), (), 0, shape[axis]) for axis in range(len(shape))]
    values = values.at[tuple(spot)].set(least)
    longest = shape.index(max(shape))
    spot[longest] = (spot[longest] + 1) % shape[longest]
    return values.at[tuple(spot)].set(largest)


def block_scale(stream_key, extent, split, least, high):
    gain, own = 1.0, jax.random.fold_in(stream_key, 6)
    for dim, parts in split:
        heights = jnp.exp(jax.random.uniform(jax.random.fold_in(own, dim), (parts,), jnp.float32, least / len(split), high / len(split)))
        gain = gain * jnp.repeat(heights, extent[dim] // parts).reshape([-1 if axis == dim else 1 for axis in range(len(extent))])
    return gain


def split_up(number_of, total, limit, slope):
    portions = [(1 << 20) // math.isqrt(grade ** slope) + 1 for grade in range(2, number_of + 1)]
    rest, given = total - limit - (number_of - 1), [1] * (number_of - 1)
    while rest > 0:
        free = [i for i in range(number_of - 1) if given[i] < limit]
        mass, left = sum([portions[i] for i in free]), rest
        for i in free:
            extra = min(limit - given[i], max(1, left * portions[i] // mass), rest)
            given[i] = given[i] + extra
            rest = rest - extra
    return np.array([limit] + given)


def ragged_sizes(own_key, amount, total, most, lean):
    if amount == 2:
        one = jax.random.randint(own_key, (), max(1, total - most), min(most, total - 1) + 1)
        return jnp.stack([one, total - one])
    sizes = jnp.asarray(split_up(amount, total, most, lean), jnp.int32)
    pairs = (amount - 1) // 2
    giver, receiver = sizes[1:1 + 2 * pairs:2], sizes[2:2 + 2 * pairs:2]
    margin = jnp.minimum(giver - 1, most - receiver)
    moved = jax.random.randint(jax.random.fold_in(own_key, 1), (pairs,), 0, 1 << 20) % (margin + 1)
    sizes = sizes.at[1:1 + 2 * pairs:2].set(giver - moved).at[2:2 + 2 * pairs:2].set(receiver + moved)
    return sizes[jax.random.permutation(jax.random.fold_in(own_key, 2), amount)]


def scatter_about(own_key, shape, spread, most, shards=(), kind=jnp.bfloat16):
    drawn = jax.random.normal(own_key, shape, jnp.float32) * spread
    if len(shards) > 0:
        drawn = block_scale(own_key, shape, shards, -0.22, 0.18) * drawn
    return jnp.clip(drawn, min=-most, max=most).astype(kind)


def setup_inputs(seed: int = 0) -> dict:
    keys = jax.random.split(jax.random.key(seed), 8)
    return {
        "object_field": scatter_about(keys[0], (SLICES, 2, ROWS, COLS), 0.7, 4.0, ((2, 8),), jnp.float32),
        "probe": scatter_about(keys[1], (MODES, 2, WIN, WIN), 0.7, 4.0, ((0, 4),), jnp.float32),
        "measured": jnp.clip(16.0 * jax.random.uniform(keys[2], (POSITIONS, WIN, WIN), jnp.float32) ** block_scale(keys[2], (POSITIONS, WIN, WIN), ((0, 8),), -0.2, 0.2), 0.0, 16.0),
        "prop_phase": jnp.clip(jax.random.uniform(keys[3], (WIN, WIN), jnp.float32, -3.140625, 3.140625), -3.140625, 3.140625),
        "counts": ragged_sizes(keys[4], N_TILE, N_TILE * CAP // 2, CAP, 2).astype(jnp.int32),
        "row_offset": with_ends(jax.random.randint(keys[5], (POSITIONS,), 0, TILE_ROWS), jax.random.fold_in(keys[5], 1), 0, TILE_ROWS - 1).astype(jnp.int32),
        "col_offset": with_ends(jax.random.randint(keys[6], (POSITIONS,), 0, COLS - WIN + 1), jax.random.fold_in(keys[6], 1), 0, COLS - WIN).astype(jnp.int32),
    }


def forward_two(field):
    return jnp.fft.fft2(field, norm="ortho")


def inverse_two(field):
    return jnp.fft.ifft2(field, norm="ortho")


def reference(object_field, probe, measured, prop_phase, counts, row_offset, col_offset):
    layers = object_field.shape[0]
    padded = jnp.pad(object_field, ((0, 0), (0, 0), (0, WIN), (0, 0)))
    obj_wave = lax.complex(padded[:, 0], padded[:, 1])
    probe_wave = lax.complex(probe[:, 0], probe[:, 1])
    kernel = lax.complex(jnp.cos(prop_phase), jnp.sin(prop_phase))
    slot_ids = jnp.arange(N_TILE * CAP, dtype=jnp.int32)
    owners = slot_ids // CAP
    live = ((slot_ids % CAP) < counts[owners]).astype(object_field.dtype)
    rows_start = (owners * TILE_ROWS + row_offset).astype(jnp.int32)
    zero_index = jnp.zeros((), jnp.int32)

    def visit(carry, inputs):
        grad_obj, grad_probe = carry
        row_start, col_start, alive, target = inputs
        start = (zero_index, row_start.astype(jnp.int32), col_start.astype(jnp.int32))
        window = lax.dynamic_slice(obj_wave, start, (layers, WIN, WIN))
        wave = probe_wave * window[0]
        before = []
        for layer in range(1, layers):
            moved = inverse_two(kernel * forward_two(wave))
            before.append(moved)
            wave = moved * window[layer]
        far_field = forward_two(wave)
        intensity = jnp.sum(jnp.real(far_field) ** 2 + jnp.imag(far_field) ** 2, axis=0)
        weight = (intensity - target) / MODES * alive
        back = inverse_two(weight * far_field)
        pieces = [None] * layers
        for layer in range(layers - 1, 0, -1):
            pieces[layer] = jnp.sum(jnp.conj(before[layer - 1]) * back, axis=0)
            back = inverse_two(jnp.conj(kernel) * forward_two(jnp.conj(window[layer]) * back))
        pieces[0] = jnp.sum(jnp.conj(probe_wave) * back, axis=0)
        grad_probe = grad_probe + jnp.conj(window[0]) * back
        current = lax.dynamic_slice(grad_obj, start, (layers, WIN, WIN))
        grad_obj = lax.dynamic_update_slice(grad_obj, current + jnp.stack(pieces), start)
        return (grad_obj, grad_probe), None

    init = (jnp.zeros_like(obj_wave), jnp.zeros_like(probe_wave))
    (grad_obj, grad_probe), _ = lax.scan(visit, init, (rows_start, col_offset, live, measured))
    grad_obj = grad_obj[:, :N_TILE * TILE_ROWS]
    object_grad = jnp.stack([jnp.real(grad_obj), jnp.imag(grad_obj)], axis=1).astype(jnp.float32)
    probe_grad = jnp.stack([jnp.real(grad_probe), jnp.imag(grad_probe)], axis=1).astype(jnp.float32)
    return object_grad, probe_grad
```

```python
import functools
import math

import jax
import jax.numpy as jnp
from jax import lax
from jax.experimental import pallas as pl
from jax.experimental.pallas import tpu as pltpu
from jax.sharding import PartitionSpec as P

F32 = jnp.float32
BF16 = jnp.bfloat16
VMEM_SPEC = pl.BlockSpec(memory_space=pltpu.VMEM)


def shifted(block, axis, distance):
    devices = range(lax.axis_size(axis))
    route = [(i - distance, i) for i in devices if i - distance in devices]
    return lax.ppermute(block, axis, route)


def dft_tables(length):
    indices = jnp.arange(length, dtype=jnp.int32)
    product = indices[:, None] * indices[None, :] % length
    angle = product.astype(F32) * (2.0 * math.pi / length)
    factor = 1.0 / math.sqrt(length)
    cosine, sine = jnp.cos(angle) * factor, jnp.sin(angle) * factor

    def parts(x):
        high = lax.reduce_precision(x, 8, 7)
        return high.astype(BF16), (x - high).astype(BF16)

    c_hi, c_lo = parts(cosine)
    s_hi, s_lo = parts(sine)
    plus_hi = jnp.block([[c_hi, -s_hi], [s_hi, c_hi]])
    plus_lo = jnp.block([[c_lo, -s_lo], [s_lo, c_lo]])
    minus_hi = jnp.block([[c_hi, s_hi], [-s_hi, c_hi]])
    minus_lo = jnp.block([[c_lo, s_lo], [-s_lo, c_lo]])
    left = jnp.stack([
        jnp.concatenate([minus_hi, minus_hi, minus_lo], axis=1),
        jnp.concatenate([plus_hi, plus_hi, plus_lo], axis=1),
    ])
    right = jnp.stack([
        jnp.concatenate([plus_hi, plus_hi, plus_lo], axis=0),
        jnp.concatenate([minus_hi, minus_hi, minus_lo], axis=0),
    ])
    return left, right


def split(x, axis):
    high = x.astype(BF16)
    low = (x - high.astype(F32)).astype(BF16)
    return jnp.concatenate([high, low, high], axis=axis)


def transform(real, imag, left_ref, right_ref, way):
    n = real.shape[0]
    stacked = split(jnp.concatenate([real, imag], axis=0), 0)
    mid = jnp.dot(left_ref[way], stacked, preferred_element_type=F32)
    wide = split(jnp.concatenate([mid[:n], mid[n:]], axis=1), 1)
    out = jnp.dot(wide, right_ref[way], preferred_element_type=F32)
    return out[:, :n], out[:, n:]


def times(a, b):
    return a[0] * b[0] - a[1] * b[1], a[0] * b[1] + a[1] * b[0]


def times_conj(a, b):
    return a[0] * b[0] + a[1] * b[1], a[0] * b[1] - a[1] * b[0]


def cut_windows(own_ref, next_ref, ext_ref, window_ref, row, col, first):
    layers, _, tile_rows, columns = own_ref.shape
    width = window_ref.shape[-1]

    @pl.when(first)
    def _():
        ext_ref[:, :, :tile_rows, :] = own_ref[...]
        ext_ref[:, :, tile_rows:, :] = next_ref[...]

    base = pl.multiple_of(row // 8 * 8, 8)
    extra = row - base
    turn = lax.rem(columns - col, columns)
    for layer in range(layers):
        for part in range(2):
            block = ext_ref[layer, part, pl.ds(base, width + 8), :]
            block = pltpu.roll(block, lax.rem(width + 8 - extra, width + 8), 0)[:width]
            window_ref[layer, part] = pltpu.roll(block, turn, 1)[:, :width]


def forward_kernel(count_ref, row_ref, col_ref, own_ref, next_ref, probe_ref, prop_ref, left_ref, right_ref,
                   before_ref, far_ref, power_ref, ext_ref, window_ref):
    slot, mode = pl.program_id(0), pl.program_id(1)
    alive = slot < count_ref[0]

    @pl.when(mode == 0)
    def _():
        cut_windows(own_ref, next_ref, ext_ref, window_ref, row_ref[slot], col_ref[slot], slot == 0)
        power_ref[...] = jnp.zeros_like(power_ref)

    @pl.when(alive)
    def _():
        wave = times((probe_ref[mode, 0], probe_ref[mode, 1]), (window_ref[0, 0], window_ref[0, 1]))
        spectrum = transform(*wave, left_ref, right_ref, 0)
        moved = transform(*times((prop_ref[0], prop_ref[1]), spectrum), left_ref, right_ref, 1)
        before_ref[0, 0, 0] = moved[0]
        before_ref[0, 0, 1] = moved[1]
        wave = times(moved, (window_ref[1, 0], window_ref[1, 1]))
        far = transform(*wave, left_ref, right_ref, 0)
        far_ref[0, 0, 0] = far[0]
        far_ref[0, 0, 1] = far[1]
        power_ref[0] += far[0] * far[0] + far[1] * far[1]


def backward_kernel(count_ref, row_ref, col_ref, own_ref, next_ref, probe_ref, prop_ref, left_ref, right_ref,
                    before_ref, far_ref, power_ref, measured_ref,
                    grad_ref, rim_ref, probe_grad_ref, ext_ref, window_ref, piece_ref, total_ref, *, modes):
    slot, mode = pl.program_id(0), pl.program_id(1)
    local_modes = pl.num_programs(1)
    alive = slot < count_ref[0]
    layers, _, tile_rows, columns = own_ref.shape
    width = window_ref.shape[-1]

    @pl.when((slot == 0) & (mode == 0))
    def _():
        total_ref[...] = jnp.zeros_like(total_ref)
        probe_grad_ref[...] = jnp.zeros_like(probe_grad_ref)

    @pl.when(mode == 0)
    def _():
        cut_windows(own_ref, next_ref, ext_ref, window_ref, row_ref[slot], col_ref[slot], slot == 0)
        piece_ref[...] = jnp.zeros_like(piece_ref)

    @pl.when(alive)
    def _():
        weight = (power_ref[0] - measured_ref[0]) / modes
        back = transform(weight * far_ref[0, 0, 0], weight * far_ref[0, 0, 1], left_ref, right_ref, 1)
        term = times_conj((before_ref[0, 0, 0], before_ref[0, 0, 1]), back)
        piece_ref[1, 0] += term[0]
        piece_ref[1, 1] += term[1]
        inner = transform(*times_conj((window_ref[1, 0], window_ref[1, 1]), back), left_ref, right_ref, 0)
        back = transform(*times_conj((prop_ref[0], prop_ref[1]), inner), left_ref, right_ref, 1)
        term = times_conj((probe_ref[mode, 0], probe_ref[mode, 1]), back)
        piece_ref[0, 0] += term[0]
        piece_ref[0, 1] += term[1]
        term = times_conj((window_ref[0, 0], window_ref[0, 1]), back)
        probe_grad_ref[mode, 0] += term[0]
        probe_grad_ref[mode, 1] += term[1]

    @pl.when(alive & (mode == local_modes - 1))
    def _():
        row, col = row_ref[slot], col_ref[slot]
        base = pl.multiple_of(row // 8 * 8, 8)
        extra = row - base
        for layer in range(layers):
            for part in range(2):
                block = piece_ref[layer, part]
                block = jnp.concatenate([block, jnp.zeros((width, columns - width), F32)], axis=1)
                block = pltpu.roll(block, col, 1)
                block = jnp.concatenate([block, jnp.zeros((8, columns), F32)], axis=0)
                block = pltpu.roll(block, extra, 0)
                total_ref[layer, part, pl.ds(base, width + 8), :] += block

    @pl.when((slot == pl.num_programs(0) - 1) & (mode == local_modes - 1))
    def _():
        grad_ref[...] = total_ref[:, :, :tile_rows, :]
        rim_ref[...] = total_ref[:, :, tile_rows:, :]


def per_device(object_field, probe, measured, prop_phase, counts, row_offset, col_offset):
    layers, _, tile_rows, columns = object_field.shape
    width = probe.shape[-1]
    local_modes = probe.shape[0]
    modes = local_modes * lax.axis_size("mode")
    slots = row_offset.shape[0]
    next_rows = shifted(object_field, "tile", -1)
    left, right = dft_tables(width)
    prop = jnp.stack([jnp.cos(prop_phase), jnp.sin(prop_phase)])

    per_mode = pl.BlockSpec((1, 1, 2, width, width), lambda s, m, *_: (s, m, 0, 0, 0))
    per_slot = pl.BlockSpec((1, width, width), lambda s, m, *_: (s, 0, 0))
    ext_shape = pltpu.VMEM((layers, 2, tile_rows + width, columns), F32)
    window_shape = pltpu.VMEM((layers, 2, width, width), F32)
    field = jax.ShapeDtypeStruct((slots, local_modes, 2, width, width), F32)
    params = pltpu.CompilerParams(dimension_semantics=("arbitrary", "arbitrary"), vmem_limit_bytes=60 << 20)

    before, far, local_power = pl.pallas_call(
        forward_kernel,
        out_shape=(field, field, jax.ShapeDtypeStruct((slots, width, width), F32)),
        grid_spec=pltpu.PrefetchScalarGridSpec(
            num_scalar_prefetch=3,
            grid=(slots, local_modes),
            in_specs=[VMEM_SPEC] * 6,
            out_specs=(per_mode, per_mode, per_slot),
            scratch_shapes=[ext_shape, window_shape],
        ),
        compiler_params=params,
        name="forward",
    )(counts, row_offset, col_offset, object_field, next_rows, probe, prop, left, right)

    power = lax.psum(local_power, "mode")

    whole = lambda shape: pl.BlockSpec(shape, lambda s, m, *_: (0,) * len(shape))
    grad, rim, grad_probe = pl.pallas_call(
        functools.partial(backward_kernel, modes=modes),
        out_shape=(
            jax.ShapeDtypeStruct(object_field.shape, F32),
            jax.ShapeDtypeStruct((layers, 2, width, columns), F32),
            jax.ShapeDtypeStruct(probe.shape, F32),
        ),
        grid_spec=pltpu.PrefetchScalarGridSpec(
            num_scalar_prefetch=3,
            grid=(slots, local_modes),
            in_specs=[VMEM_SPEC] * 6 + [per_mode, per_mode, per_slot, per_slot],
            out_specs=(whole(object_field.shape), whole((layers, 2, width, columns)), whole(probe.shape)),
            scratch_shapes=[ext_shape, window_shape, window_shape, ext_shape],
        ),
        compiler_params=params,
        name="backward",
    )(counts, row_offset, col_offset, object_field, next_rows, probe, prop, left, right, before, far, power, measured)

    arrived = shifted(rim, "tile", 1)
    object_grad = lax.psum(grad.at[:, :, :width, :].add(arrived), "mode")
    probe_grad = lax.psum(grad_probe, "tile")
    return (object_grad, probe_grad)


def solution(mesh):
    placed = (
        P(None, None, "tile", None),
        P("mode", None, None, None),
        P("tile", None, None),
        P(),
        P("tile"),
        P("tile"),
        P("tile"),
    )
    return jax.shard_map(
        per_device,
        mesh=mesh,
        in_specs=placed,
        out_specs=(P(None, None, "tile", None), P("mode", None, None, None)),
        check_vma=False,
    )
```

```python
import functools
import math

import jax
import jax.numpy as jnp
import numpy as np
from jax import lax
from jax.experimental import pallas as pl
from jax.experimental.pallas import tpu as pltpu
from jax.sharding import PartitionSpec as P

F32 = jnp.float32
BF16 = jnp.bfloat16
MESH = pl.DeviceIdType.MESH
BLOCKS = 8
VMEM_SPEC = pl.BlockSpec(memory_space=pltpu.VMEM)


def shifted(block, axis, distance):
    devices = range(lax.axis_size(axis))
    route = [(i - distance, i) for i in devices if i - distance in devices]
    return lax.ppermute(block, axis, route)


def dft_constants(length):
    indices = np.arange(length)
    angle = (indices[:, None] * indices[None, :] % length) * (2.0 * math.pi / length)
    rows = []
    for table in (np.cos(angle) / math.sqrt(length), np.sin(angle) / math.sqrt(length)):
        high = table.astype(BF16)
        rows += [high, (table - high.astype(np.float64)).astype(BF16)]
    return np.stack(rows)


def build_tables(dft_ref, left_ref, right_ref):
    n = dft_ref.shape[-1]
    for place, low in enumerate((0, 0, 1)):
        cosine, sine = dft_ref[low], dft_ref[2 + low]
        for way in range(2):
            upper, lower = (sine, -sine) if way == 0 else (-sine, sine)
            at = 2 * n * place
            left_ref[way, :n, at:at + n] = cosine
            left_ref[way, :n, at + n:at + 2 * n] = upper
            left_ref[way, n:, at:at + n] = lower
            left_ref[way, n:, at + n:at + 2 * n] = cosine
            right_ref[way, at:at + n, :n] = cosine
            right_ref[way, at:at + n, n:] = lower
            right_ref[way, at + n:at + 2 * n, :n] = upper
            right_ref[way, at + n:at + 2 * n, n:] = cosine


def split(x, axis):
    high = x.astype(BF16)
    low = (x - high.astype(F32)).astype(BF16)
    return jnp.concatenate([high, low, high], axis=axis)


def transform(real, imag, left_ref, right_ref, way):
    n = real.shape[0]
    stacked = split(jnp.concatenate([real, imag], axis=0), 0)
    mid = jnp.dot(left_ref[way], stacked, preferred_element_type=F32)
    wide = split(jnp.concatenate([mid[:n], mid[n:]], axis=1), 1)
    out = jnp.dot(wide, right_ref[way], preferred_element_type=F32)
    return out[:, :n], out[:, n:]


def times(a, b):
    return a[0] * b[0] - a[1] * b[1], a[0] * b[1] + a[1] * b[0]


def times_conj(a, b):
    return a[0] * b[0] + a[1] * b[1], a[0] * b[1] - a[1] * b[0]


def cut_windows(own_ref, next_ref, ext_ref, window_ref, row, col, first):
    layers, _, tile_rows, columns = own_ref.shape
    width = window_ref.shape[-1]

    @pl.when(first)
    def _():
        ext_ref[:, :, :tile_rows, :] = own_ref[...]
        ext_ref[:, :, tile_rows:, :] = next_ref[...]

    base = pl.multiple_of(row // 8 * 8, 8)
    extra = row - base
    turn = lax.rem(columns - col, columns)
    for layer in range(layers):
        for part in range(2):
            block = ext_ref[layer, part, pl.ds(base, width + 8), :]
            block = pltpu.roll(block, lax.rem(width + 8 - extra, width + 8), 0)[:width]
            window_ref[layer, part] = pltpu.roll(block, turn, 1)[:, :width]


def forward_kernel(count_ref, row_ref, col_ref, own_ref, next_ref, probe_ref, prop_ref, dft_ref,
                   before_ref, far_ref, power_ref, ext_ref, window_ref, left_ref, right_ref):
    slot, mode = pl.program_id(0), pl.program_id(1)
    alive = slot < count_ref[0]

    @pl.when((slot == 0) & (mode == 0))
    def _():
        build_tables(dft_ref, left_ref, right_ref)

    @pl.when(mode == 0)
    def _():
        cut_windows(own_ref, next_ref, ext_ref, window_ref, row_ref[slot], col_ref[slot], slot == 0)
        power_ref[...] = jnp.zeros_like(power_ref)

    @pl.when(alive)
    def _():
        wave = times((probe_ref[mode, 0], probe_ref[mode, 1]), (window_ref[0, 0], window_ref[0, 1]))
        spectrum = transform(*wave, left_ref, right_ref, 0)
        moved = transform(*times((prop_ref[0], prop_ref[1]), spectrum), left_ref, right_ref, 1)
        before_ref[0, 0, 0] = moved[0]
        before_ref[0, 0, 1] = moved[1]
        wave = times(moved, (window_ref[1, 0], window_ref[1, 1]))
        far = transform(*wave, left_ref, right_ref, 0)
        far_ref[0, 0, 0] = far[0]
        far_ref[0, 0, 1] = far[1]
        power_ref[0] += far[0] * far[0] + far[1] * far[1]


def backward_kernel(count_ref, row_ref, col_ref, own_ref, next_ref, probe_ref, prop_ref, dft_ref,
                    before_ref, far_ref, power_ref, measured_ref,
                    grad_ref, rim_ref, probe_grad_ref, ext_ref, window_ref, piece_ref, total_ref, left_ref, right_ref, *, modes):
    slot, mode = pl.program_id(0), pl.program_id(1)
    local_modes = pl.num_programs(1)
    alive = slot < count_ref[0]
    layers, _, tile_rows, columns = own_ref.shape
    width = window_ref.shape[-1]

    @pl.when((slot == 0) & (mode == 0))
    def _():
        build_tables(dft_ref, left_ref, right_ref)
        total_ref[...] = jnp.zeros_like(total_ref)
        probe_grad_ref[...] = jnp.zeros_like(probe_grad_ref)

    @pl.when(mode == 0)
    def _():
        cut_windows(own_ref, next_ref, ext_ref, window_ref, row_ref[slot], col_ref[slot], slot == 0)
        piece_ref[...] = jnp.zeros_like(piece_ref)

    @pl.when(alive)
    def _():
        weight = (power_ref[0] - measured_ref[0]) / modes
        back = transform(weight * far_ref[0, 0, 0], weight * far_ref[0, 0, 1], left_ref, right_ref, 1)
        term = times_conj((before_ref[0, 0, 0], before_ref[0, 0, 1]), back)
        piece_ref[1, 0] += term[0]
        piece_ref[1, 1] += term[1]
        inner = transform(*times_conj((window_ref[1, 0], window_ref[1, 1]), back), left_ref, right_ref, 0)
        back = transform(*times_conj((prop_ref[0], prop_ref[1]), inner), left_ref, right_ref, 1)
        term = times_conj((probe_ref[mode, 0], probe_ref[mode, 1]), back)
        piece_ref[0, 0] += term[0]
        piece_ref[0, 1] += term[1]
        term = times_conj((window_ref[0, 0], window_ref[0, 1]), back)
        probe_grad_ref[mode, 0] += term[0]
        probe_grad_ref[mode, 1] += term[1]

    @pl.when(alive & (mode == local_modes - 1))
    def _():
        row, col = row_ref[slot], col_ref[slot]
        base = pl.multiple_of(row // 8 * 8, 8)
        extra = row - base
        for layer in range(layers):
            for part in range(2):
                block = piece_ref[layer, part]
                block = jnp.concatenate([block, jnp.zeros((width, columns - width), F32)], axis=1)
                block = pltpu.roll(block, col, 1)
                block = jnp.concatenate([block, jnp.zeros((8, columns), F32)], axis=0)
                block = pltpu.roll(block, extra, 0)
                total_ref[layer, part, pl.ds(base, width + 8), :] += block

    @pl.when((slot == pl.num_programs(0) - 1) & (mode == local_modes - 1))
    def _():
        grad_ref[...] = total_ref[:, :, :tile_rows, :]
        rim_ref[...] = total_ref[:, :, tile_rows:, :]


class Line:
    def __init__(self, own, out_ref, up_ref, down_ref, send_ref, sems):
        self.own, self.out, self.up, self.down, self.send = own, out_ref, up_ref, down_ref, send_ref
        self.sems = sems
        self.n = lax.axis_size("mode")
        self.blocks = out_ref.shape[0]
        place = lax.axis_index("mode")
        left = place < self.n // 2
        self.depth = jnp.where(left, place, self.n - 1 - place)
        self.inward = jnp.where(left, place + 1, place - 1)
        self.outward = jnp.where(left, place - 1, place + 1)
        self.middle = self.depth == self.n // 2 - 1
        self.inner = self.depth > 0

    def copy(self, source, target, sent, received, device, k):
        return pltpu.make_async_remote_copy(
            src_ref=source.at[k], dst_ref=target.at[k],
            send_sem=self.sems.at[sent, k], recv_sem=self.sems.at[received, k],
            device_id={"mode": device}, device_id_type=MESH)

    def in_up(self, k):
        return self.copy(self.send, self.up, 0, 2, self.inward, k)

    def in_across(self, k):
        return self.copy(self.send, self.down, 0, 3, self.inward, k)

    def out_down(self, k):
        return self.copy(self.out, self.down, 1, 3, self.outward, k)

    def greet(self, barrier):
        pl.semaphore_signal(barrier, inc=1, device_id={"mode": self.inward}, device_id_type=MESH)

        @pl.when(self.inner)
        def _():
            pl.semaphore_signal(barrier, inc=1, device_id={"mode": self.outward}, device_id_type=MESH)

        return jnp.where(self.inner, 2, 1)

    def gather(self, k):
        @pl.when(self.inner)
        def _():
            self.in_up(k).wait_recv()
            self.send[k] = self.own(k) + self.up[k]

        @pl.when(jnp.logical_not(self.inner))
        def _():
            self.send[k] = self.own(k)

        @pl.when(self.middle)
        def _():
            self.in_across(k).start()

        @pl.when(jnp.logical_not(self.middle))
        def _():
            self.in_up(k).start()

    def spread(self, k, middle):
        self.in_across(k).wait_recv()
        self.out[k] = self.send[k] + self.down[k] if middle else self.down[k]

        @pl.when(self.inner)
        def _():
            self.out_down(k).start()

    def step(self, t):
        if t < self.blocks:
            self.gather(t)
        if 0 <= t - 1 < self.blocks:
            @pl.when(self.middle)
            def _():
                self.spread(t - 1, True)
        late = t - (self.n - 1)
        if 0 <= late < self.blocks:
            @pl.when(jnp.logical_not(self.middle))
            def _():
                self.spread(late, False)

    def steps(self):
        return self.blocks + self.n - 1

    def drain(self):
        for k in range(self.blocks):
            self.in_up(k).wait_send()

        @pl.when(self.inner)
        def _():
            for k in range(self.blocks):
                self.out_down(k).wait_send()


def mode_sum_kernel(in_ref, out_ref, up_ref, down_ref, send_ref, sems):
    line = Line(lambda k: in_ref[k], out_ref, up_ref, down_ref, send_ref, sems)
    barrier = pltpu.get_barrier_semaphore()
    pl.semaphore_wait(barrier, line.greet(barrier))
    for t in range(line.steps()):
        line.step(t)
    line.drain()


def sum_over_mode(local):
    shape = local.shape
    blocked = local.reshape(BLOCKS, -1, shape[-1])
    buffer = pltpu.VMEM(blocked.shape, F32)
    return pl.pallas_call(
        mode_sum_kernel,
        out_shape=jax.ShapeDtypeStruct(blocked.shape, F32),
        in_specs=[VMEM_SPEC],
        out_specs=VMEM_SPEC,
        scratch_shapes=[buffer, buffer, buffer, pltpu.SemaphoreType.DMA((4, BLOCKS))],
        compiler_params=pltpu.CompilerParams(collective_id=0, has_side_effects=True, vmem_limit_bytes=60 << 20),
        name="mode_sum",
    )(blocked).reshape(shape)


def finish_kernel(grad_ref, rim_ref, probe_ref, out_ref, probe_out_ref,
                  up_ref, down_ref, send_ref, rim_in_ref, part_ref, got_ref, sems, rim_sems, probe_sems):
    tiles = lax.axis_size("tile")
    me = lax.axis_index("tile")
    bits = tiles.bit_length() - 1
    has_next, has_last = me < tiles - 1, me > 0

    def rim_copy(k):
        return pltpu.make_async_remote_copy(
            src_ref=rim_ref.at[k], dst_ref=rim_in_ref.at[k],
            send_sem=rim_sems.at[0, k], recv_sem=rim_sems.at[1, k],
            device_id={"tile": me + 1}, device_id_type=MESH)

    def own(k):
        return send_ref[k]

    line = Line(own, out_ref, up_ref, down_ref, send_ref, sems)

    def other(bit):
        low = lax.rem(me // (1 << bit), 2)
        return me + (1 - 2 * low) * (1 << bit)

    side = lax.rem(me, 2)

    def probe_copy(step, source, target):
        return pltpu.make_async_remote_copy(
            src_ref=source, dst_ref=target,
            send_sem=probe_sems.at[0, step], recv_sem=probe_sems.at[1, step],
            device_id={"tile": other(0 if step == bits else step)}, device_id_type=MESH)

    def exchange(step):
        if step == 0:
            return probe_copy(0, probe_ref.at[1 - side], got_ref.at[0])
        if step < bits:
            return probe_copy(step, part_ref.at[step - 1], got_ref.at[step])
        return probe_copy(step, part_ref.at[bits - 1], probe_out_ref.at[side])

    barrier = pltpu.get_barrier_semaphore()
    count = line.greet(barrier)
    for bit in range(bits):
        pl.semaphore_signal(barrier, inc=1, device_id={"tile": other(bit)}, device_id_type=MESH)

    @pl.when(has_next)
    def _():
        pl.semaphore_signal(barrier, inc=1, device_id={"tile": me + 1}, device_id_type=MESH)

    @pl.when(has_last)
    def _():
        pl.semaphore_signal(barrier, inc=1, device_id={"tile": me - 1}, device_id_type=MESH)

    pl.semaphore_wait(barrier, count + bits + has_next.astype(jnp.int32) + has_last.astype(jnp.int32))

    exchange(0).start()

    @pl.when(has_next)
    def _():
        for k in range(line.blocks):
            rim_copy(k).start()

    for t in range(line.steps()):
        if t < line.blocks:
            @pl.when(has_last)
            def _():
                rim_copy(t).wait_recv()
                send_ref[t] = grad_ref[t] + rim_in_ref[t]

            @pl.when(jnp.logical_not(has_last))
            def _():
                send_ref[t] = grad_ref[t]
        line.step(t)
        bit = (t - 1) // 3
        if t % 3 == 1 and bit < bits:
            exchange(bit).wait_recv()
            part_ref[bit] = (probe_ref[side] if bit == 0 else part_ref[bit - 1]) + got_ref[bit]
            exchange(bit + 1).start()
    probe_out_ref[side] = part_ref[bits - 1]
    exchange(bits).wait_recv()
    for step in range(bits + 1):
        exchange(step).wait_send()
    line.drain()

    @pl.when(has_next)
    def _():
        for k in range(line.blocks):
            rim_copy(k).wait_send()


def finish(grad, rim, grad_probe):
    bits = lax.axis_size("tile").bit_length() - 1
    blocked = (BLOCKS, -1, grad.shape[-1])
    own, edge = grad.reshape(blocked), rim.reshape(blocked)
    halves = grad_probe.reshape(2, -1, grad_probe.shape[-1])
    buffer = pltpu.VMEM(own.shape, F32)
    parts = pltpu.VMEM((bits, *halves.shape[1:]), F32)
    object_grad, probe_grad = pl.pallas_call(
        finish_kernel,
        out_shape=(jax.ShapeDtypeStruct(own.shape, F32), jax.ShapeDtypeStruct(halves.shape, F32)),
        in_specs=[VMEM_SPEC] * 3,
        out_specs=(VMEM_SPEC, VMEM_SPEC),
        scratch_shapes=[buffer, buffer, buffer, buffer, parts, parts,
                        pltpu.SemaphoreType.DMA((4, BLOCKS)), pltpu.SemaphoreType.DMA((2, BLOCKS)),
                        pltpu.SemaphoreType.DMA((2, bits + 1))],
        compiler_params=pltpu.CompilerParams(collective_id=1, has_side_effects=True, vmem_limit_bytes=60 << 20),
        name="finish",
    )(own, edge, halves)
    return object_grad.reshape(grad.shape), probe_grad.reshape(grad_probe.shape)


def per_device(object_field, probe, measured, prop_phase, counts, row_offset, col_offset):
    layers, _, tile_rows, columns = object_field.shape
    width = probe.shape[-1]
    local_modes = probe.shape[0]
    modes = local_modes * lax.axis_size("mode")
    slots = row_offset.shape[0]
    next_rows = shifted(object_field, "tile", -1)
    dft = jnp.asarray(dft_constants(width))
    prop = jnp.stack([jnp.cos(prop_phase), jnp.sin(prop_phase)])

    per_mode = pl.BlockSpec((1, 1, 2, width, width), lambda s, m, *_: (s, m, 0, 0, 0))
    per_slot = pl.BlockSpec((1, width, width), lambda s, m, *_: (s, 0, 0))
    ext_shape = pltpu.VMEM((layers, 2, tile_rows + width, columns), F32)
    window_shape = pltpu.VMEM((layers, 2, width, width), F32)
    table_shapes = [pltpu.VMEM((2, 2 * width, 6 * width), BF16), pltpu.VMEM((2, 6 * width, 2 * width), BF16)]
    field = jax.ShapeDtypeStruct((slots, local_modes, 2, width, width), F32)
    params = pltpu.CompilerParams(dimension_semantics=("arbitrary", "arbitrary"), vmem_limit_bytes=60 << 20)

    before, far, local_power = pl.pallas_call(
        forward_kernel,
        out_shape=(field, field, jax.ShapeDtypeStruct((slots, width, width), F32)),
        grid_spec=pltpu.PrefetchScalarGridSpec(
            num_scalar_prefetch=3,
            grid=(slots, local_modes),
            in_specs=[VMEM_SPEC] * 5,
            out_specs=(per_mode, per_mode, per_slot),
            scratch_shapes=[ext_shape, window_shape, *table_shapes],
        ),
        compiler_params=params,
        name="forward",
    )(counts, row_offset, col_offset, object_field, next_rows, probe, prop, dft)

    power = sum_over_mode(local_power)

    whole = lambda shape: pl.BlockSpec(shape, lambda s, m, *_: (0,) * len(shape))
    grad, rim, grad_probe = pl.pallas_call(
        functools.partial(backward_kernel, modes=modes),
        out_shape=(
            jax.ShapeDtypeStruct(object_field.shape, F32),
            jax.ShapeDtypeStruct((layers, 2, width, columns), F32),
            jax.ShapeDtypeStruct(probe.shape, F32),
        ),
        grid_spec=pltpu.PrefetchScalarGridSpec(
            num_scalar_prefetch=3,
            grid=(slots, local_modes),
            in_specs=[VMEM_SPEC] * 5 + [per_mode, per_mode, per_slot, per_slot],
            out_specs=(whole(object_field.shape), whole((layers, 2, width, columns)), whole(probe.shape)),
            scratch_shapes=[ext_shape, window_shape, window_shape, ext_shape, *table_shapes],
        ),
        compiler_params=params,
        name="backward",
    )(counts, row_offset, col_offset, object_field, next_rows, probe, prop, dft, before, far, power, measured)

    return finish(grad, rim, grad_probe)


def solution(mesh):
    placed = (
        P(None, None, "tile", None),
        P("mode", None, None, None),
        P("tile", None, None),
        P(),
        P("tile"),
        P("tile"),
        P("tile"),
    )
    return jax.shard_map(
        per_device,
        mesh=mesh,
        in_specs=placed,
        out_specs=(P(None, None, "tile", None), P("mode", None, None, None)),
        check_vma=False,
    )
```

```python
import functools
import math

import jax
import jax.numpy as jnp
import numpy as np
from jax import lax
from jax.experimental import pallas as pl
from jax.experimental.pallas import tpu as pltpu
from jax.sharding import PartitionSpec as P

F32 = jnp.float32
BF16 = jnp.bfloat16
MESH = pl.DeviceIdType.MESH
BLOCKS = 8
VMEM_SPEC = pl.BlockSpec(memory_space=pltpu.VMEM)


def shifted(block, axis, distance):
    devices = range(lax.axis_size(axis))
    route = [(i - distance, i) for i in devices if i - distance in devices]
    return lax.ppermute(block, axis, route)


def dft_constants(length):
    half = length // 2
    n, k = np.arange(half)[:, None], np.arange(half)[None, :]
    sides = []
    for side in ("left", "right"):
        for way in range(2):
            for parity in range(2):
                angle = (n * (2 * k + parity) % length) * (2.0 * math.pi / length)
                real = np.cos(angle) / math.sqrt(length)
                imag = (-np.sin(angle) if way == 0 else np.sin(angle)) / math.sqrt(length)
                if (side == "left") == (way == 0):
                    real, imag = real.T, imag.T
                if side == "left":
                    table = np.block([[real, -imag], [imag, real]])
                else:
                    table = np.block([[real, imag], [-imag, real]])
                high = table.astype(BF16)
                sides += [high, (table - high.astype(np.float64)).astype(BF16)]
    return np.stack(sides).reshape(2, 2, 2, 2, length, length)


def build_tables(dft_ref, left_ref, right_ref):
    n = dft_ref.shape[-1]
    for place, low in enumerate((0, 0, 1)):
        for way in range(2):
            for parity in range(2):
                left_ref[way, parity, :, place * n:(place + 1) * n] = dft_ref[0, way, parity, low]
                right_ref[way, parity, place * n:(place + 1) * n, :] = dft_ref[1, way, parity, low]


def split(x, axis):
    high = x.astype(BF16)
    low = (x - high.astype(F32)).astype(BF16)
    return jnp.concatenate([high, low, high], axis=axis)


def one_side(real, imag, product, axis, way):
    half = real.shape[axis] // 2
    first = lambda x: lax.slice_in_dim(x, 0, half, axis=axis)
    second = lambda x: lax.slice_in_dim(x, half, 2 * half, axis=axis)
    join = lambda x, y: jnp.concatenate([x, y], axis=axis)
    if way == 0:
        even = product(split(join(first(real) + second(real), first(imag) + second(imag)), axis), 0)
        odd = product(split(join(first(real) - second(real), first(imag) - second(imag)), axis), 1)
        return join(first(even), first(odd)), join(second(even), second(odd))
    even = product(split(join(first(real), first(imag)), axis), 0)
    odd = product(split(join(second(real), second(imag)), axis), 1)
    total, rest = even + odd, even - odd
    return join(first(total), first(rest)), join(second(total), second(rest))


def transform(real, imag, left_ref, right_ref, way):
    on_left = lambda x, parity: jnp.dot(left_ref[way, parity], x, preferred_element_type=F32)
    on_right = lambda x, parity: jnp.dot(x, right_ref[way, parity], preferred_element_type=F32)
    real, imag = one_side(real, imag, on_left, 0, way)
    return one_side(real, imag, on_right, 1, way)


def to_even_odd(fields):
    n = fields.shape[-1]
    order = np.concatenate([np.arange(0, n, 2), np.arange(1, n, 2)])
    pick = jnp.asarray(np.eye(n, dtype=np.float32)[order])
    high = lax.Precision.HIGHEST
    fields = jnp.einsum("ajk,lk->ajl", fields, pick, precision=high)
    return jnp.einsum("ij,ajl->ail", pick, fields, precision=high)


def times(a, b):
    return a[0] * b[0] - a[1] * b[1], a[0] * b[1] + a[1] * b[0]


def times_conj(a, b):
    return a[0] * b[0] + a[1] * b[1], a[0] * b[1] - a[1] * b[0]


def cut_windows(own_ref, next_ref, ext_ref, window_ref, row, col, first):
    layers, _, tile_rows, columns = own_ref.shape
    width = window_ref.shape[-1]

    @pl.when(first)
    def _():
        ext_ref[:, :, :tile_rows, :] = own_ref[...]
        ext_ref[:, :, tile_rows:, :] = next_ref[...]

    base = pl.multiple_of(row // 8 * 8, 8)
    extra = row - base
    turn = lax.rem(columns - col, columns)
    for layer in range(layers):
        for part in range(2):
            block = ext_ref[layer, part, pl.ds(base, width + 8), :]
            block = pltpu.roll(block, lax.rem(width + 8 - extra, width + 8), 0)[:width]
            window_ref[layer, part] = pltpu.roll(block, turn, 1)[:, :width]


def forward_kernel(count_ref, row_ref, col_ref, own_ref, next_ref, probe_ref, prop_ref, dft_ref,
                   before_ref, far_ref, power_ref, window_out_ref, ext_ref, left_ref, right_ref):
    window_ref = window_out_ref.at[0]
    slot, mode = pl.program_id(0), pl.program_id(1)
    alive = slot < count_ref[0]

    @pl.when((slot == 0) & (mode == 0))
    def _():
        build_tables(dft_ref, left_ref, right_ref)

    @pl.when((mode == 0) & alive)
    def _():
        cut_windows(own_ref, next_ref, ext_ref, window_ref, row_ref[slot], col_ref[slot], slot == 0)

    @pl.when(mode == 0)
    def _():
        power_ref[...] = jnp.zeros_like(power_ref)

    @pl.when(alive)
    def _():
        wave = times((probe_ref[mode, 0], probe_ref[mode, 1]), (window_ref[0, 0], window_ref[0, 1]))
        spectrum = transform(*wave, left_ref, right_ref, 0)
        moved = transform(*times((prop_ref[0], prop_ref[1]), spectrum), left_ref, right_ref, 1)
        before_ref[0, 0, 0] = moved[0]
        before_ref[0, 0, 1] = moved[1]
        wave = times(moved, (window_ref[1, 0], window_ref[1, 1]))
        far = transform(*wave, left_ref, right_ref, 0)
        far_ref[0, 0, 0] = far[0]
        far_ref[0, 0, 1] = far[1]
        power_ref[0] += far[0] * far[0] + far[1] * far[1]


def backward_kernel(count_ref, row_ref, col_ref, probe_ref, prop_ref, dft_ref,
                    before_ref, far_ref, power_ref, measured_ref, window_in_ref,
                    grad_ref, rim_ref, probe_grad_ref, piece_ref, total_ref, left_ref, right_ref, *, modes):
    window_ref = window_in_ref.at[0]
    slot, mode = pl.program_id(0), pl.program_id(1)
    local_modes = pl.num_programs(1)
    alive = slot < count_ref[0]
    layers, _, tile_rows, columns = grad_ref.shape
    width = piece_ref.shape[-1]

    @pl.when((slot == 0) & (mode == 0))
    def _():
        build_tables(dft_ref, left_ref, right_ref)
        total_ref[...] = jnp.zeros_like(total_ref)
        probe_grad_ref[...] = jnp.zeros_like(probe_grad_ref)

    @pl.when(mode == 0)
    def _():
        piece_ref[...] = jnp.zeros_like(piece_ref)

    @pl.when(alive)
    def _():
        weight = (power_ref[0] - measured_ref[0]) / modes
        back = transform(weight * far_ref[0, 0, 0], weight * far_ref[0, 0, 1], left_ref, right_ref, 1)
        term = times_conj((before_ref[0, 0, 0], before_ref[0, 0, 1]), back)
        piece_ref[1, 0] += term[0]
        piece_ref[1, 1] += term[1]
        inner = transform(*times_conj((window_ref[1, 0], window_ref[1, 1]), back), left_ref, right_ref, 0)
        back = transform(*times_conj((prop_ref[0], prop_ref[1]), inner), left_ref, right_ref, 1)
        term = times_conj((probe_ref[mode, 0], probe_ref[mode, 1]), back)
        piece_ref[0, 0] += term[0]
        piece_ref[0, 1] += term[1]
        term = times_conj((window_ref[0, 0], window_ref[0, 1]), back)
        probe_grad_ref[mode, 0] += term[0]
        probe_grad_ref[mode, 1] += term[1]

    @pl.when(alive & (mode == local_modes - 1))
    def _():
        row, col = row_ref[slot], col_ref[slot]
        base = pl.multiple_of(row // 8 * 8, 8)
        extra = row - base
        for layer in range(layers):
            for part in range(2):
                block = piece_ref[layer, part]
                block = jnp.concatenate([block, jnp.zeros((width, columns - width), F32)], axis=1)
                block = pltpu.roll(block, col, 1)
                block = jnp.concatenate([block, jnp.zeros((8, columns), F32)], axis=0)
                block = pltpu.roll(block, extra, 0)
                total_ref[layer, part, pl.ds(base, width + 8), :] += block

    @pl.when((slot == pl.num_programs(0) - 1) & (mode == local_modes - 1))
    def _():
        grad_ref[...] = total_ref[:, :, :tile_rows, :]
        rim_ref[...] = total_ref[:, :, tile_rows:, :]


class Line:
    def __init__(self, own, out_ref, up_ref, down_ref, send_ref, sems):
        self.own, self.out, self.up, self.down, self.send = own, out_ref, up_ref, down_ref, send_ref
        self.sems = sems
        self.n = lax.axis_size("mode")
        self.blocks = out_ref.shape[0]
        place = lax.axis_index("mode")
        left = place < self.n // 2
        self.depth = jnp.where(left, place, self.n - 1 - place)
        self.inward = jnp.where(left, place + 1, place - 1)
        self.outward = jnp.where(left, place - 1, place + 1)
        self.middle = self.depth == self.n // 2 - 1
        self.inner = self.depth > 0

    def copy(self, source, target, sent, received, device, k):
        return pltpu.make_async_remote_copy(
            src_ref=source.at[k], dst_ref=target.at[k],
            send_sem=self.sems.at[sent, k], recv_sem=self.sems.at[received, k],
            device_id={"mode": device}, device_id_type=MESH)

    def in_up(self, k):
        return self.copy(self.send, self.up, 0, 2, self.inward, k)

    def in_across(self, k):
        return self.copy(self.send, self.down, 0, 3, self.inward, k)

    def out_down(self, k):
        return self.copy(self.out, self.down, 1, 3, self.outward, k)

    def greet(self, barrier):
        pl.semaphore_signal(barrier, inc=1, device_id={"mode": self.inward}, device_id_type=MESH)

        @pl.when(self.inner)
        def _():
            pl.semaphore_signal(barrier, inc=1, device_id={"mode": self.outward}, device_id_type=MESH)

        return jnp.where(self.inner, 2, 1)

    def gather(self, k):
        @pl.when(self.inner)
        def _():
            self.in_up(k).wait_recv()
            self.send[k] = self.own(k) + self.up[k]

        @pl.when(jnp.logical_not(self.inner))
        def _():
            self.send[k] = self.own(k)

        @pl.when(self.middle)
        def _():
            self.in_across(k).start()

        @pl.when(jnp.logical_not(self.middle))
        def _():
            self.in_up(k).start()

    def spread(self, k, middle):
        self.in_across(k).wait_recv()
        self.out[k] = self.send[k] + self.down[k] if middle else self.down[k]

        @pl.when(self.inner)
        def _():
            self.out_down(k).start()

    def step(self, t):
        if t < self.blocks:
            self.gather(t)
        if 0 <= t - 1 < self.blocks:
            @pl.when(self.middle)
            def _():
                self.spread(t - 1, True)
        late = t - (self.n - 1)
        if 0 <= late < self.blocks:
            @pl.when(jnp.logical_not(self.middle))
            def _():
                self.spread(late, False)

    def steps(self):
        return self.blocks + self.n - 1

    def drain(self):
        for k in range(self.blocks):
            self.in_up(k).wait_send()

        @pl.when(self.inner)
        def _():
            for k in range(self.blocks):
                self.out_down(k).wait_send()


def mode_sum_kernel(in_ref, out_ref, up_ref, down_ref, send_ref, sems):
    line = Line(lambda k: in_ref[k], out_ref, up_ref, down_ref, send_ref, sems)
    barrier = pltpu.get_barrier_semaphore()
    pl.semaphore_wait(barrier, line.greet(barrier))
    for t in range(line.steps()):
        line.step(t)
    line.drain()


def sum_over_mode(local):
    shape = local.shape
    blocked = local.reshape(BLOCKS, -1, shape[-1])
    buffer = pltpu.VMEM(blocked.shape, F32)
    return pl.pallas_call(
        mode_sum_kernel,
        out_shape=jax.ShapeDtypeStruct(blocked.shape, F32),
        in_specs=[VMEM_SPEC],
        out_specs=VMEM_SPEC,
        scratch_shapes=[buffer, buffer, buffer, pltpu.SemaphoreType.DMA((4, BLOCKS))],
        compiler_params=pltpu.CompilerParams(collective_id=0, has_side_effects=True, vmem_limit_bytes=60 << 20),
        name="mode_sum",
    )(blocked).reshape(shape)


def finish_kernel(grad_ref, rim_ref, probe_ref, out_ref, probe_out_ref,
                  up_ref, down_ref, send_ref, rim_in_ref, part_ref, got_ref, sems, rim_sems, probe_sems):
    tiles = lax.axis_size("tile")
    me = lax.axis_index("tile")
    bits = tiles.bit_length() - 1
    has_next, has_last = me < tiles - 1, me > 0

    def rim_copy(k):
        return pltpu.make_async_remote_copy(
            src_ref=rim_ref.at[k], dst_ref=rim_in_ref.at[k],
            send_sem=rim_sems.at[0, k], recv_sem=rim_sems.at[1, k],
            device_id={"tile": me + 1}, device_id_type=MESH)

    def own(k):
        return send_ref[k]

    line = Line(own, out_ref, up_ref, down_ref, send_ref, sems)

    def other(bit):
        low = lax.rem(me // (1 << bit), 2)
        return me + (1 - 2 * low) * (1 << bit)

    side = lax.rem(me, 2)

    def probe_copy(step, source, target):
        return pltpu.make_async_remote_copy(
            src_ref=source, dst_ref=target,
            send_sem=probe_sems.at[0, step], recv_sem=probe_sems.at[1, step],
            device_id={"tile": other(0 if step == bits else step)}, device_id_type=MESH)

    def exchange(step):
        if step == 0:
            return probe_copy(0, probe_ref.at[1 - side], got_ref.at[0])
        if step < bits:
            return probe_copy(step, part_ref.at[step - 1], got_ref.at[step])
        return probe_copy(step, part_ref.at[bits - 1], probe_out_ref.at[side])

    barrier = pltpu.get_barrier_semaphore()
    count = line.greet(barrier)
    for bit in range(bits):
        pl.semaphore_signal(barrier, inc=1, device_id={"tile": other(bit)}, device_id_type=MESH)

    @pl.when(has_next)
    def _():
        pl.semaphore_signal(barrier, inc=1, device_id={"tile": me + 1}, device_id_type=MESH)

    @pl.when(has_last)
    def _():
        pl.semaphore_signal(barrier, inc=1, device_id={"tile": me - 1}, device_id_type=MESH)

    pl.semaphore_wait(barrier, count + bits + has_next.astype(jnp.int32) + has_last.astype(jnp.int32))

    exchange(0).start()

    @pl.when(has_next)
    def _():
        for k in range(line.blocks):
            rim_copy(k).start()

    for t in range(line.steps()):
        if t < line.blocks:
            @pl.when(has_last)
            def _():
                rim_copy(t).wait_recv()
                send_ref[t] = grad_ref[t] + rim_in_ref[t]

            @pl.when(jnp.logical_not(has_last))
            def _():
                send_ref[t] = grad_ref[t]
        line.step(t)
        bit = (t - 1) // 3
        if t % 3 == 1 and bit < bits:
            exchange(bit).wait_recv()
            part_ref[bit] = (probe_ref[side] if bit == 0 else part_ref[bit - 1]) + got_ref[bit]
            exchange(bit + 1).start()
    probe_out_ref[side] = part_ref[bits - 1]
    exchange(bits).wait_recv()
    for step in range(bits + 1):
        exchange(step).wait_send()
    line.drain()

    @pl.when(has_next)
    def _():
        for k in range(line.blocks):
            rim_copy(k).wait_send()


def finish(grad, rim, grad_probe):
    bits = lax.axis_size("tile").bit_length() - 1
    blocked = (BLOCKS, -1, grad.shape[-1])
    own, edge = grad.reshape(blocked), rim.reshape(blocked)
    halves = grad_probe.reshape(2, -1, grad_probe.shape[-1])
    buffer = pltpu.VMEM(own.shape, F32)
    parts = pltpu.VMEM((bits, *halves.shape[1:]), F32)
    object_grad, probe_grad = pl.pallas_call(
        finish_kernel,
        out_shape=(jax.ShapeDtypeStruct(own.shape, F32), jax.ShapeDtypeStruct(halves.shape, F32)),
        in_specs=[VMEM_SPEC] * 3,
        out_specs=(VMEM_SPEC, VMEM_SPEC),
        scratch_shapes=[buffer, buffer, buffer, buffer, parts, parts,
                        pltpu.SemaphoreType.DMA((4, BLOCKS)), pltpu.SemaphoreType.DMA((2, BLOCKS)),
                        pltpu.SemaphoreType.DMA((2, bits + 1))],
        compiler_params=pltpu.CompilerParams(collective_id=1, has_side_effects=True, vmem_limit_bytes=60 << 20),
        name="finish",
    )(own, edge, halves)
    return object_grad.reshape(grad.shape), probe_grad.reshape(grad_probe.shape)


def per_device(object_field, probe, measured, prop_phase, counts, row_offset, col_offset):
    layers, _, tile_rows, columns = object_field.shape
    width = probe.shape[-1]
    local_modes = probe.shape[0]
    modes = local_modes * lax.axis_size("mode")
    slots = row_offset.shape[0]
    next_rows = shifted(object_field, "tile", -1)
    dft = jnp.asarray(dft_constants(width))
    spectral = jnp.concatenate([jnp.cos(prop_phase)[None], jnp.sin(prop_phase)[None], measured])
    spectral = to_even_odd(spectral)
    prop, measured = spectral[:2], spectral[2:]

    per_mode = pl.BlockSpec((1, 1, 2, width, width), lambda s, m, *_: (s, m, 0, 0, 0))
    per_slot = pl.BlockSpec((1, width, width), lambda s, m, *_: (s, 0, 0))
    ext_shape = pltpu.VMEM((layers, 2, tile_rows + width, columns), F32)
    window_shape = pltpu.VMEM((layers, 2, width, width), F32)
    table_shapes = [pltpu.VMEM((2, 2, width, 3 * width), BF16), pltpu.VMEM((2, 2, 3 * width, width), BF16)]
    per_window = pl.BlockSpec((1, layers, 2, width, width), lambda s, m, *_: (s, 0, 0, 0, 0))
    field = jax.ShapeDtypeStruct((slots, local_modes, 2, width, width), F32)
    params = pltpu.CompilerParams(dimension_semantics=("arbitrary", "arbitrary"), vmem_limit_bytes=60 << 20)

    before, far, local_power, windows = pl.pallas_call(
        forward_kernel,
        out_shape=(field, field, jax.ShapeDtypeStruct((slots, width, width), F32),
                   jax.ShapeDtypeStruct((slots, layers, 2, width, width), F32)),
        grid_spec=pltpu.PrefetchScalarGridSpec(
            num_scalar_prefetch=3,
            grid=(slots, local_modes),
            in_specs=[VMEM_SPEC] * 5,
            out_specs=(per_mode, per_mode, per_slot, per_window),
            scratch_shapes=[ext_shape, *table_shapes],
        ),
        compiler_params=params,
        name="forward",
    )(counts, row_offset, col_offset, object_field, next_rows, probe, prop, dft)

    power = sum_over_mode(local_power)

    whole = lambda shape: pl.BlockSpec(shape, lambda s, m, *_: (0,) * len(shape))
    grad, rim, grad_probe = pl.pallas_call(
        functools.partial(backward_kernel, modes=modes),
        out_shape=(
            jax.ShapeDtypeStruct(object_field.shape, F32),
            jax.ShapeDtypeStruct((layers, 2, width, columns), F32),
            jax.ShapeDtypeStruct(probe.shape, F32),
        ),
        grid_spec=pltpu.PrefetchScalarGridSpec(
            num_scalar_prefetch=3,
            grid=(slots, local_modes),
            in_specs=[VMEM_SPEC] * 3 + [per_mode, per_mode, per_slot, per_slot, per_window],
            out_specs=(whole(object_field.shape), whole((layers, 2, width, columns)), whole(probe.shape)),
            scratch_shapes=[window_shape, ext_shape, *table_shapes],
        ),
        compiler_params=params,
        name="backward",
    )(counts, row_offset, col_offset, probe, prop, dft, before, far, power, measured, windows)

    return finish(grad, rim, grad_probe)


def solution(mesh):
    placed = (
        P(None, None, "tile", None),
        P("mode", None, None, None),
        P("tile", None, None),
        P(),
        P("tile"),
        P("tile"),
        P("tile"),
    )
    return jax.shard_map(
        per_device,
        mesh=mesh,
        in_specs=placed,
        out_specs=(P(None, None, "tile", None), P("mode", None, None, None)),
        check_vma=False,
    )
```

```python
import functools
import math

import jax
import jax.numpy as jnp
import numpy as np
from jax import lax
from jax.experimental import pallas as pl
from jax.experimental.pallas import tpu as pltpu
from jax.sharding import PartitionSpec as P

F32 = jnp.float32
BF16 = jnp.bfloat16
MESH = pl.DeviceIdType.MESH
BLOCKS = 16
VMEM_SPEC = pl.BlockSpec(memory_space=pltpu.VMEM)


def shifted(block, axis, distance):
    devices = range(lax.axis_size(axis))
    route = [(i - distance, i) for i in devices if i - distance in devices]
    return lax.ppermute(block, axis, route)


def dft_constants(length):
    half = length // 2
    n, k = np.arange(half)[:, None], np.arange(half)[None, :]
    sides = []
    for side in ("left", "right"):
        for way in range(2):
            for parity in range(2):
                angle = (n * (2 * k + parity) % length) * (2.0 * math.pi / length)
                real = np.cos(angle) / math.sqrt(length)
                imag = (-np.sin(angle) if way == 0 else np.sin(angle)) / math.sqrt(length)
                if (side == "left") == (way == 0):
                    real, imag = real.T, imag.T
                if side == "left":
                    table = np.block([[real, -imag], [imag, real]])
                else:
                    table = np.block([[real, imag], [-imag, real]])
                high = table.astype(BF16)
                sides += [high, (table - high.astype(np.float64)).astype(BF16)]
    return np.stack(sides).reshape(2, 2, 2, 2, length, length)


def build_tables(dft_ref, left_ref, right_ref):
    n = dft_ref.shape[-1]
    for place, low in enumerate((0, 0, 1)):
        for way in range(2):
            for parity in range(2):
                left_ref[way, parity, :, place * n:(place + 1) * n] = dft_ref[0, way, parity, low]
                right_ref[way, parity, place * n:(place + 1) * n, :] = dft_ref[1, way, parity, low]


def split(x, axis):
    high = x.astype(BF16)
    low = (x - high.astype(F32)).astype(BF16)
    return jnp.concatenate([high, low, high], axis=axis)


def one_side(real, imag, product, axis, way):
    half = real.shape[axis] // 2
    first = lambda x: lax.slice_in_dim(x, 0, half, axis=axis)
    second = lambda x: lax.slice_in_dim(x, half, 2 * half, axis=axis)
    join = lambda x, y: jnp.concatenate([x, y], axis=axis)
    if way == 0:
        even = product(split(join(first(real) + second(real), first(imag) + second(imag)), axis), 0)
        odd = product(split(join(first(real) - second(real), first(imag) - second(imag)), axis), 1)
        return join(first(even), first(odd)), join(second(even), second(odd))
    even = product(split(join(first(real), first(imag)), axis), 0)
    odd = product(split(join(second(real), second(imag)), axis), 1)
    total, rest = even + odd, even - odd
    return join(first(total), first(rest)), join(second(total), second(rest))


def transform(real, imag, left_ref, right_ref, way):
    on_left = lambda x, parity: jnp.dot(left_ref[way, parity], x, preferred_element_type=F32)
    on_right = lambda x, parity: jnp.dot(x, right_ref[way, parity], preferred_element_type=F32)
    real, imag = one_side(real, imag, on_left, 0, way)
    return one_side(real, imag, on_right, 1, way)


def to_even_odd(fields):
    n = fields.shape[-1]
    order = np.concatenate([np.arange(0, n, 2), np.arange(1, n, 2)])
    pick = jnp.asarray(np.eye(n, dtype=np.float32)[order])
    high = lax.Precision.HIGHEST
    fields = jnp.einsum("ajk,lk->ajl", fields, pick, precision=high)
    return jnp.einsum("ij,ajl->ail", pick, fields, precision=high)


def times(a, b):
    return a[0] * b[0] - a[1] * b[1], a[0] * b[1] + a[1] * b[0]


def times_conj(a, b):
    return a[0] * b[0] + a[1] * b[1], a[0] * b[1] - a[1] * b[0]


def cut_windows(own_ref, next_ref, ext_ref, window_ref, row, col, first):
    layers, _, tile_rows, columns = own_ref.shape
    width = window_ref.shape[-1]

    @pl.when(first)
    def _():
        ext_ref[:, :, :tile_rows, :] = own_ref[...]
        ext_ref[:, :, tile_rows:, :] = next_ref[...]

    base = pl.multiple_of(row // 8 * 8, 8)
    extra = row - base
    turn = lax.rem(columns - col, columns)
    for layer in range(layers):
        for part in range(2):
            block = ext_ref[layer, part, pl.ds(base, width + 8), :]
            block = pltpu.roll(block, lax.rem(width + 8 - extra, width + 8), 0)[:width]
            window_ref[layer, part] = pltpu.roll(block, turn, 1)[:, :width]


def forward_kernel(count_ref, row_ref, col_ref, own_ref, next_ref, probe_ref, prop_ref, dft_ref,
                   before_ref, far_ref, power_ref, window_out_ref, ext_ref, left_ref, right_ref):
    window_ref = window_out_ref.at[0]
    slot, mode = pl.program_id(0), pl.program_id(1)
    alive = slot < count_ref[0]

    @pl.when((slot == 0) & (mode == 0))
    def _():
        build_tables(dft_ref, left_ref, right_ref)

    @pl.when((mode == 0) & alive)
    def _():
        cut_windows(own_ref, next_ref, ext_ref, window_ref, row_ref[slot], col_ref[slot], slot == 0)

    @pl.when(mode == 0)
    def _():
        power_ref[...] = jnp.zeros_like(power_ref)

    @pl.when(alive)
    def _():
        wave = times((probe_ref[mode, 0], probe_ref[mode, 1]), (window_ref[0, 0], window_ref[0, 1]))
        spectrum = transform(*wave, left_ref, right_ref, 0)
        moved = transform(*times((prop_ref[0], prop_ref[1]), spectrum), left_ref, right_ref, 1)
        before_ref[0, 0, 0] = moved[0]
        before_ref[0, 0, 1] = moved[1]
        wave = times(moved, (window_ref[1, 0], window_ref[1, 1]))
        far = transform(*wave, left_ref, right_ref, 0)
        far_ref[0, 0, 0] = far[0]
        far_ref[0, 0, 1] = far[1]
        power_ref[0] += far[0] * far[0] + far[1] * far[1]


def backward_kernel(count_ref, row_ref, col_ref, probe_ref, prop_ref, dft_ref,
                    before_ref, far_ref, power_ref, measured_ref, window_in_ref,
                    grad_ref, rim_ref, probe_grad_ref, piece_ref, total_ref, left_ref, right_ref, *, modes):
    window_ref = window_in_ref.at[0]
    slot, mode = pl.program_id(0), pl.program_id(1)
    local_modes = pl.num_programs(1)
    alive = slot < count_ref[0]
    layers, _, tile_rows, columns = grad_ref.shape
    width = piece_ref.shape[-1]

    @pl.when((slot == 0) & (mode == 0))
    def _():
        build_tables(dft_ref, left_ref, right_ref)
        total_ref[...] = jnp.zeros_like(total_ref)
        probe_grad_ref[...] = jnp.zeros_like(probe_grad_ref)

    @pl.when(mode == 0)
    def _():
        piece_ref[...] = jnp.zeros_like(piece_ref)

    @pl.when(alive)
    def _():
        weight = (power_ref[0] - measured_ref[0]) / modes
        back = transform(weight * far_ref[0, 0, 0], weight * far_ref[0, 0, 1], left_ref, right_ref, 1)
        term = times_conj((before_ref[0, 0, 0], before_ref[0, 0, 1]), back)
        piece_ref[1, 0] += term[0]
        piece_ref[1, 1] += term[1]
        inner = transform(*times_conj((window_ref[1, 0], window_ref[1, 1]), back), left_ref, right_ref, 0)
        back = transform(*times_conj((prop_ref[0], prop_ref[1]), inner), left_ref, right_ref, 1)
        term = times_conj((probe_ref[mode, 0], probe_ref[mode, 1]), back)
        piece_ref[0, 0] += term[0]
        piece_ref[0, 1] += term[1]
        term = times_conj((window_ref[0, 0], window_ref[0, 1]), back)
        probe_grad_ref[mode, 0] += term[0]
        probe_grad_ref[mode, 1] += term[1]

    @pl.when(alive & (mode == local_modes - 1))
    def _():
        row, col = row_ref[slot], col_ref[slot]
        base = pl.multiple_of(row // 8 * 8, 8)
        extra = row - base
        for layer in range(layers):
            for part in range(2):
                block = piece_ref[layer, part]
                block = jnp.concatenate([block, jnp.zeros((width, columns - width), F32)], axis=1)
                block = pltpu.roll(block, col, 1)
                block = jnp.concatenate([block, jnp.zeros((8, columns), F32)], axis=0)
                block = pltpu.roll(block, extra, 0)
                total_ref[layer, part, pl.ds(base, width + 8), :] += block

    @pl.when((slot == pl.num_programs(0) - 1) & (mode == local_modes - 1))
    def _():
        grad_ref[...] = total_ref[:, :, :tile_rows, :]
        rim_ref[...] = total_ref[:, :, tile_rows:, :]


class Line:
    def __init__(self, own, out_ref, up_ref, down_ref, send_ref, sems):
        self.own, self.out, self.up, self.down, self.send = own, out_ref, up_ref, down_ref, send_ref
        self.sems = sems
        self.n = lax.axis_size("mode")
        self.blocks = out_ref.shape[0]
        place = lax.axis_index("mode")
        left = place < self.n // 2
        self.depth = jnp.where(left, place, self.n - 1 - place)
        self.inward = jnp.where(left, place + 1, place - 1)
        self.outward = jnp.where(left, place - 1, place + 1)
        self.middle = self.depth == self.n // 2 - 1
        self.inner = self.depth > 0

    def copy(self, source, target, sent, received, device, k):
        return pltpu.make_async_remote_copy(
            src_ref=source.at[k], dst_ref=target.at[k],
            send_sem=self.sems.at[sent, k], recv_sem=self.sems.at[received, k],
            device_id={"mode": device}, device_id_type=MESH)

    def in_up(self, k):
        return self.copy(self.send, self.up, 0, 2, self.inward, k)

    def in_across(self, k):
        return self.copy(self.send, self.down, 0, 3, self.inward, k)

    def out_down(self, k):
        return self.copy(self.out, self.down, 1, 3, self.outward, k)

    def greet(self, barrier):
        pl.semaphore_signal(barrier, inc=1, device_id={"mode": self.inward}, device_id_type=MESH)

        @pl.when(self.inner)
        def _():
            pl.semaphore_signal(barrier, inc=1, device_id={"mode": self.outward}, device_id_type=MESH)

        return jnp.where(self.inner, 2, 1)

    def gather(self, k):
        @pl.when(self.inner)
        def _():
            self.in_up(k).wait_recv()
            self.send[k] = self.own(k) + self.up[k]

        @pl.when(jnp.logical_not(self.inner))
        def _():
            self.send[k] = self.own(k)

        @pl.when(self.middle)
        def _():
            self.in_across(k).start()

        @pl.when(jnp.logical_not(self.middle))
        def _():
            self.in_up(k).start()

    def spread(self, k, middle):
        self.in_across(k).wait_recv()
        self.out[k] = self.send[k] + self.down[k] if middle else self.down[k]

        @pl.when(self.inner)
        def _():
            self.out_down(k).start()

    def step(self, t):
        if t < self.blocks:
            self.gather(t)
        if 0 <= t - 2 < self.blocks:
            @pl.when(self.middle)
            def _():
                self.spread(t - 2, True)
        late = t - self.blocks
        if 0 <= late < self.blocks:
            @pl.when(jnp.logical_not(self.middle))
            def _():
                self.spread(late, False)

    def steps(self):
        return 2 * self.blocks

    def drain(self):
        for k in range(self.blocks):
            self.in_up(k).wait_send()

        @pl.when(self.inner)
        def _():
            for k in range(self.blocks):
                self.out_down(k).wait_send()


def mode_sum_kernel(in_ref, out_ref, up_ref, down_ref, send_ref, sems):
    line = Line(lambda k: in_ref[k], out_ref, up_ref, down_ref, send_ref, sems)
    barrier = pltpu.get_barrier_semaphore()
    pl.semaphore_wait(barrier, line.greet(barrier))
    for t in range(line.steps()):
        line.step(t)
    line.drain()


def sum_over_mode(local):
    shape = local.shape
    blocked = local.reshape(BLOCKS, -1, shape[-1])
    buffer = pltpu.VMEM(blocked.shape, F32)
    return pl.pallas_call(
        mode_sum_kernel,
        out_shape=jax.ShapeDtypeStruct(blocked.shape, F32),
        in_specs=[VMEM_SPEC],
        out_specs=VMEM_SPEC,
        scratch_shapes=[buffer, buffer, buffer, pltpu.SemaphoreType.DMA((4, BLOCKS))],
        compiler_params=pltpu.CompilerParams(collective_id=0, has_side_effects=True, vmem_limit_bytes=60 << 20),
        name="mode_sum",
    )(blocked).reshape(shape)


def finish_kernel(grad_ref, rim_ref, probe_ref, out_ref, probe_out_ref,
                  up_ref, down_ref, send_ref, rim_in_ref, part_ref, got_ref, sems, rim_sems, probe_sems):
    tiles = lax.axis_size("tile")
    me = lax.axis_index("tile")
    bits = tiles.bit_length() - 1
    has_next, has_last = me < tiles - 1, me > 0

    def rim_copy(k):
        return pltpu.make_async_remote_copy(
            src_ref=rim_ref.at[k], dst_ref=rim_in_ref.at[k],
            send_sem=rim_sems.at[0, k], recv_sem=rim_sems.at[1, k],
            device_id={"tile": me + 1}, device_id_type=MESH)

    def own(k):
        return send_ref[k]

    line = Line(own, out_ref, up_ref, down_ref, send_ref, sems)

    def other(bit):
        low = lax.rem(me // (1 << bit), 2)
        return me + (1 - 2 * low) * (1 << bit)

    side = lax.rem(me, 2)

    def probe_copy(step, source, target):
        return pltpu.make_async_remote_copy(
            src_ref=source, dst_ref=target,
            send_sem=probe_sems.at[0, step], recv_sem=probe_sems.at[1, step],
            device_id={"tile": other(0 if step == bits else step)}, device_id_type=MESH)

    def exchange(step):
        if step == 0:
            return probe_copy(0, probe_ref.at[1 - side], got_ref.at[0])
        if step < bits:
            return probe_copy(step, part_ref.at[step - 1], got_ref.at[step])
        return probe_copy(step, part_ref.at[bits - 1], probe_out_ref.at[side])

    barrier = pltpu.get_barrier_semaphore()
    count = line.greet(barrier)
    for bit in range(bits):
        pl.semaphore_signal(barrier, inc=1, device_id={"tile": other(bit)}, device_id_type=MESH)

    @pl.when(has_next)
    def _():
        pl.semaphore_signal(barrier, inc=1, device_id={"tile": me + 1}, device_id_type=MESH)

    @pl.when(has_last)
    def _():
        pl.semaphore_signal(barrier, inc=1, device_id={"tile": me - 1}, device_id_type=MESH)

    pl.semaphore_wait(barrier, count + bits + has_next.astype(jnp.int32) + has_last.astype(jnp.int32))

    exchange(0).start()

    @pl.when(has_next)
    def _():
        for k in range(line.blocks):
            rim_copy(k).start()

    for t in range(line.steps()):
        if t < line.blocks:
            @pl.when(has_last)
            def _():
                rim_copy(t).wait_recv()
                send_ref[t] = grad_ref[t] + rim_in_ref[t]

            @pl.when(jnp.logical_not(has_last))
            def _():
                send_ref[t] = grad_ref[t]
        line.step(t)
        bit = 0 if t == 1 else (t - 4) // 5
        if t == 1 or (t % 5 == 4 and 0 < bit < bits):
            exchange(bit).wait_recv()
            part_ref[bit] = (probe_ref[side] if bit == 0 else part_ref[bit - 1]) + got_ref[bit]
            exchange(bit + 1).start()
    probe_out_ref[side] = part_ref[bits - 1]
    exchange(bits).wait_recv()
    for step in range(bits + 1):
        exchange(step).wait_send()
    line.drain()

    @pl.when(has_next)
    def _():
        for k in range(line.blocks):
            rim_copy(k).wait_send()


def finish(grad, rim, grad_probe):
    bits = lax.axis_size("tile").bit_length() - 1
    blocked = (BLOCKS, -1, grad.shape[-1])
    own, edge = grad.reshape(blocked), rim.reshape(blocked)
    halves = grad_probe.reshape(2, -1, grad_probe.shape[-1])
    buffer = pltpu.VMEM(own.shape, F32)
    parts = pltpu.VMEM((bits, *halves.shape[1:]), F32)
    object_grad, probe_grad = pl.pallas_call(
        finish_kernel,
        out_shape=(jax.ShapeDtypeStruct(own.shape, F32), jax.ShapeDtypeStruct(halves.shape, F32)),
        in_specs=[VMEM_SPEC] * 3,
        out_specs=(VMEM_SPEC, VMEM_SPEC),
        scratch_shapes=[buffer, buffer, buffer, buffer, parts, parts,
                        pltpu.SemaphoreType.DMA((4, BLOCKS)), pltpu.SemaphoreType.DMA((2, BLOCKS)),
                        pltpu.SemaphoreType.DMA((2, bits + 1))],
        compiler_params=pltpu.CompilerParams(collective_id=1, has_side_effects=True, vmem_limit_bytes=60 << 20),
        name="finish",
    )(own, edge, halves)
    return object_grad.reshape(grad.shape), probe_grad.reshape(grad_probe.shape)


def per_device(object_field, probe, measured, prop_phase, counts, row_offset, col_offset):
    layers, _, tile_rows, columns = object_field.shape
    width = probe.shape[-1]
    local_modes = probe.shape[0]
    modes = local_modes * lax.axis_size("mode")
    slots = row_offset.shape[0]
    next_rows = shifted(object_field, "tile", -1)
    dft = jnp.asarray(dft_constants(width))
    spectral = jnp.concatenate([jnp.cos(prop_phase)[None], jnp.sin(prop_phase)[None], measured])
    spectral = to_even_odd(spectral)
    prop, measured = spectral[:2], spectral[2:]

    per_mode = pl.BlockSpec((1, 1, 2, width, width), lambda s, m, *_: (s, m, 0, 0, 0))
    per_slot = pl.BlockSpec((1, width, width), lambda s, m, *_: (s, 0, 0))
    ext_shape = pltpu.VMEM((layers, 2, tile_rows + width, columns), F32)
    window_shape = pltpu.VMEM((layers, 2, width, width), F32)
    table_shapes = [pltpu.VMEM((2, 2, width, 3 * width), BF16), pltpu.VMEM((2, 2, 3 * width, width), BF16)]
    per_window = pl.BlockSpec((1, layers, 2, width, width), lambda s, m, *_: (s, 0, 0, 0, 0))
    field = jax.ShapeDtypeStruct((slots, local_modes, 2, width, width), F32)
    params = pltpu.CompilerParams(dimension_semantics=("arbitrary", "arbitrary"), vmem_limit_bytes=60 << 20)

    before, far, local_power, windows = pl.pallas_call(
        forward_kernel,
        out_shape=(field, field, jax.ShapeDtypeStruct((slots, width, width), F32),
                   jax.ShapeDtypeStruct((slots, layers, 2, width, width), F32)),
        grid_spec=pltpu.PrefetchScalarGridSpec(
            num_scalar_prefetch=3,
            grid=(slots, local_modes),
            in_specs=[VMEM_SPEC] * 5,
            out_specs=(per_mode, per_mode, per_slot, per_window),
            scratch_shapes=[ext_shape, *table_shapes],
        ),
        compiler_params=params,
        name="forward",
    )(counts, row_offset, col_offset, object_field, next_rows, probe, prop, dft)

    power = sum_over_mode(local_power)

    whole = lambda shape: pl.BlockSpec(shape, lambda s, m, *_: (0,) * len(shape))
    grad, rim, grad_probe = pl.pallas_call(
        functools.partial(backward_kernel, modes=modes),
        out_shape=(
            jax.ShapeDtypeStruct(object_field.shape, F32),
            jax.ShapeDtypeStruct((layers, 2, width, columns), F32),
            jax.ShapeDtypeStruct(probe.shape, F32),
        ),
        grid_spec=pltpu.PrefetchScalarGridSpec(
            num_scalar_prefetch=3,
            grid=(slots, local_modes),
            in_specs=[VMEM_SPEC] * 3 + [per_mode, per_mode, per_slot, per_slot, per_window],
            out_specs=(whole(object_field.shape), whole((layers, 2, width, columns)), whole(probe.shape)),
            scratch_shapes=[window_shape, ext_shape, *table_shapes],
        ),
        compiler_params=params,
        name="backward",
    )(counts, row_offset, col_offset, probe, prop, dft, before, far, power, measured, windows)

    return finish(grad, rim, grad_probe)


def solution(mesh):
    placed = (
        P(None, None, "tile", None),
        P("mode", None, None, None),
        P("tile", None, None),
        P(),
        P("tile"),
        P("tile"),
        P("tile"),
    )
    return jax.shard_map(
        per_device,
        mesh=mesh,
        in_specs=placed,
        out_specs=(P(None, None, "tile", None), P("mode", None, None, None)),
        check_vma=False,
    )
```

```python
import functools
import math

import jax
import jax.numpy as jnp
import numpy as np
from jax import lax
from jax.experimental import pallas as pl
from jax.experimental.pallas import tpu as pltpu
from jax.sharding import PartitionSpec as P

F32 = jnp.float32
BF16 = jnp.bfloat16
MESH = pl.DeviceIdType.MESH
BLOCKS = 16
VMEM_SPEC = pl.BlockSpec(memory_space=pltpu.VMEM)


def shifted(block, axis, distance):
    devices = range(lax.axis_size(axis))
    route = [(i - distance, i) for i in devices if i - distance in devices]
    return lax.ppermute(block, axis, route)


def dft_constants(length):
    half = length // 2
    n, k = np.arange(half)[:, None], np.arange(half)[None, :]
    sides = []
    for side in ("left", "right"):
        for way in range(2):
            for parity in range(2):
                angle = (n * (2 * k + parity) % length) * (2.0 * math.pi / length)
                real = np.cos(angle) / math.sqrt(length)
                imag = (-np.sin(angle) if way == 0 else np.sin(angle)) / math.sqrt(length)
                if (side == "left") == (way == 0):
                    real, imag = real.T, imag.T
                if side == "left":
                    table = np.block([[real, -imag], [imag, real]])
                else:
                    table = np.block([[real, imag], [-imag, real]])
                high = table.astype(BF16)
                sides += [high, (table - high.astype(np.float64)).astype(BF16)]
    return np.stack(sides).reshape(2, 2, 2, 2, length, length)


def build_tables(dft_ref, left_ref, right_ref):
    n = dft_ref.shape[-1]
    for place, low in enumerate((0, 0, 1)):
        for way in range(2):
            for parity in range(2):
                left_ref[way, parity, :, place * n:(place + 1) * n] = dft_ref[0, way, parity, low]
                right_ref[way, parity, place * n:(place + 1) * n, :] = dft_ref[1, way, parity, low]


def split(x, axis):
    high = x.astype(BF16)
    low = (x - high.astype(F32)).astype(BF16)
    return jnp.concatenate([high, low, high], axis=axis)


def one_side(real, imag, product, axis, way):
    half = real.shape[axis] // 2
    first = lambda x: lax.slice_in_dim(x, 0, half, axis=axis)
    second = lambda x: lax.slice_in_dim(x, half, 2 * half, axis=axis)
    join = lambda x, y: jnp.concatenate([x, y], axis=axis)
    if way == 0:
        even = product(split(join(first(real) + second(real), first(imag) + second(imag)), axis), 0)
        odd = product(split(join(first(real) - second(real), first(imag) - second(imag)), axis), 1)
        return join(first(even), first(odd)), join(second(even), second(odd))
    even = product(split(join(first(real), first(imag)), axis), 0)
    odd = product(split(join(second(real), second(imag)), axis), 1)
    total, rest = even + odd, even - odd
    return join(first(total), first(rest)), join(second(total), second(rest))


def transform(real, imag, left_ref, right_ref, way):
    on_left = lambda x, parity: jnp.dot(left_ref[way, parity], x, preferred_element_type=F32)
    on_right = lambda x, parity: jnp.dot(x, right_ref[way, parity], preferred_element_type=F32)
    real, imag = one_side(real, imag, on_left, 0, way)
    return one_side(real, imag, on_right, 1, way)


def to_even_odd(fields):
    n = fields.shape[-1]
    order = np.concatenate([np.arange(0, n, 2), np.arange(1, n, 2)])
    pick = jnp.asarray(np.eye(n, dtype=np.float32)[order])
    high = lax.Precision.HIGHEST
    fields = jnp.einsum("ajk,lk->ajl", fields, pick, precision=high)
    return jnp.einsum("ij,ajl->ail", pick, fields, precision=high)


def times(a, b):
    return a[0] * b[0] - a[1] * b[1], a[0] * b[1] + a[1] * b[0]


def times_conj(a, b):
    return a[0] * b[0] + a[1] * b[1], a[0] * b[1] - a[1] * b[0]


def cut_windows(own_ref, next_ref, ext_ref, window_ref, row, col, first):
    layers, _, tile_rows, columns = own_ref.shape
    width = window_ref.shape[-1]

    @pl.when(first)
    def _():
        ext_ref[:, :, :tile_rows, :] = own_ref[...]
        ext_ref[:, :, tile_rows:, :] = next_ref[...]

    base = pl.multiple_of(row // 8 * 8, 8)
    extra = row - base
    turn = lax.rem(columns - col, columns)
    for layer in range(layers):
        for part in range(2):
            block = ext_ref[layer, part, pl.ds(base, width + 8), :]
            block = pltpu.roll(block, lax.rem(width + 8 - extra, width + 8), 0)[:width]
            window_ref[layer, part] = pltpu.roll(block, turn, 1)[:, :width]


def forward_kernel(count_ref, row_ref, col_ref, own_ref, next_ref, probe_ref, prop_ref, dft_ref,
                   before_ref, far_ref, power_ref, window_out_ref, ext_ref, left_ref, right_ref):
    window_ref = window_out_ref.at[0]
    slot, mode = pl.program_id(0), pl.program_id(1)
    alive = slot < count_ref[0]

    @pl.when((slot == 0) & (mode == 0))
    def _():
        build_tables(dft_ref, left_ref, right_ref)

    @pl.when((mode == 0) & alive)
    def _():
        cut_windows(own_ref, next_ref, ext_ref, window_ref, row_ref[slot], col_ref[slot], slot == 0)

    @pl.when(mode == 0)
    def _():
        power_ref[...] = jnp.zeros_like(power_ref)

    @pl.when(alive)
    def _():
        wave = times((probe_ref[mode, 0], probe_ref[mode, 1]), (window_ref[0, 0], window_ref[0, 1]))
        spectrum = transform(*wave, left_ref, right_ref, 0)
        moved = transform(*times((prop_ref[0], prop_ref[1]), spectrum), left_ref, right_ref, 1)
        before_ref[0, 0, 0] = moved[0]
        before_ref[0, 0, 1] = moved[1]
        wave = times(moved, (window_ref[1, 0], window_ref[1, 1]))
        far = transform(*wave, left_ref, right_ref, 0)
        far_ref[0, 0, 0] = far[0]
        far_ref[0, 0, 1] = far[1]
        power_ref[0] += far[0] * far[0] + far[1] * far[1]


def backward_kernel(count_ref, row_ref, col_ref, probe_ref, prop_ref, dft_ref,
                    before_ref, far_ref, power_ref, measured_ref, window_in_ref,
                    grad_ref, rim_ref, probe_grad_ref, piece_ref, total_ref, left_ref, right_ref, *, modes):
    window_ref = window_in_ref.at[0]
    slot, mode = pl.program_id(0), pl.program_id(1)
    local_modes = pl.num_programs(1)
    alive = slot < count_ref[0]
    layers, _, tile_rows, columns = grad_ref.shape
    width = piece_ref.shape[-1]

    @pl.when((slot == 0) & (mode == 0))
    def _():
        build_tables(dft_ref, left_ref, right_ref)
        total_ref[...] = jnp.zeros_like(total_ref)
        probe_grad_ref[...] = jnp.zeros_like(probe_grad_ref)

    @pl.when(mode == 0)
    def _():
        piece_ref[...] = jnp.zeros_like(piece_ref)

    @pl.when(alive)
    def _():
        weight = (power_ref[0] - measured_ref[0]) / modes
        back = transform(weight * far_ref[0, 0, 0], weight * far_ref[0, 0, 1], left_ref, right_ref, 1)
        term = times_conj((before_ref[0, 0, 0], before_ref[0, 0, 1]), back)
        piece_ref[1, 0] += term[0]
        piece_ref[1, 1] += term[1]
        inner = transform(*times_conj((window_ref[1, 0], window_ref[1, 1]), back), left_ref, right_ref, 0)
        back = transform(*times_conj((prop_ref[0], prop_ref[1]), inner), left_ref, right_ref, 1)
        term = times_conj((probe_ref[mode, 0], probe_ref[mode, 1]), back)
        piece_ref[0, 0] += term[0]
        piece_ref[0, 1] += term[1]
        term = times_conj((window_ref[0, 0], window_ref[0, 1]), back)
        probe_grad_ref[mode, 0] += term[0]
        probe_grad_ref[mode, 1] += term[1]

    @pl.when(alive & (mode == local_modes - 1))
    def _():
        row, col = row_ref[slot], col_ref[slot]
        base = pl.multiple_of(row // 8 * 8, 8)
        extra = row - base
        for layer in range(layers):
            for part in range(2):
                block = piece_ref[layer, part]
                block = jnp.concatenate([block, jnp.zeros((width, columns - width), F32)], axis=1)
                block = pltpu.roll(block, col, 1)
                block = jnp.concatenate([block, jnp.zeros((8, columns), F32)], axis=0)
                block = pltpu.roll(block, extra, 0)
                total_ref[layer, part, pl.ds(base, width + 8), :] += block

    @pl.when((slot == pl.num_programs(0) - 1) & (mode == local_modes - 1))
    def _():
        grad_ref[...] = total_ref[:, :, :tile_rows, :]
        rim_ref[...] = total_ref[:, :, tile_rows:, :]


class Line:
    def __init__(self, own, out_ref, up_ref, down_ref, send_ref, sems):
        self.own, self.out, self.up, self.down, self.send = own, out_ref, up_ref, down_ref, send_ref
        self.sems = sems
        self.n = lax.axis_size("mode")
        self.blocks = out_ref.shape[0]
        place = lax.axis_index("mode")
        left = place < self.n // 2
        self.depth = jnp.where(left, place, self.n - 1 - place)
        self.inward = jnp.where(left, place + 1, place - 1)
        self.outward = jnp.where(left, place - 1, place + 1)
        self.middle = self.depth == self.n // 2 - 1
        self.inner = self.depth > 0

    def copy(self, source, target, sent, received, device, k):
        return pltpu.make_async_remote_copy(
            src_ref=source.at[k], dst_ref=target.at[k],
            send_sem=self.sems.at[sent, k], recv_sem=self.sems.at[received, k],
            device_id={"mode": device}, device_id_type=MESH)

    def in_up(self, k):
        return self.copy(self.send, self.up, 0, 2, self.inward, k)

    def in_across(self, k):
        return self.copy(self.send, self.down, 0, 3, self.inward, k)

    def out_down(self, k):
        return self.copy(self.out, self.down, 1, 3, self.outward, k)

    def greet(self, barrier):
        pl.semaphore_signal(barrier, inc=1, device_id={"mode": self.inward}, device_id_type=MESH)

        @pl.when(self.inner)
        def _():
            pl.semaphore_signal(barrier, inc=1, device_id={"mode": self.outward}, device_id_type=MESH)

        return jnp.where(self.inner, 2, 1)

    def gather(self, k):
        @pl.when(self.inner)
        def _():
            self.in_up(k).wait_recv()
            self.send[k] = self.own(k) + self.up[k]

        @pl.when(jnp.logical_not(self.inner))
        def _():
            self.send[k] = self.own(k)

        @pl.when(self.middle)
        def _():
            self.in_across(k).start()

        @pl.when(jnp.logical_not(self.middle))
        def _():
            self.in_up(k).start()

    def spread(self, k, middle):
        self.in_across(k).wait_recv()
        self.out[k] = self.send[k] + self.down[k] if middle else self.down[k]

        @pl.when(self.inner)
        def _():
            self.out_down(k).start()

    def step(self, t):
        if t < self.blocks:
            self.gather(t)
        if 0 <= t - 2 < self.blocks:
            @pl.when(self.middle)
            def _():
                self.spread(t - 2, True)
        late = t - self.blocks
        if 0 <= late < self.blocks:
            @pl.when(jnp.logical_not(self.middle))
            def _():
                self.spread(late, False)

    def steps(self):
        return 2 * self.blocks

    def drain(self):
        for k in range(self.blocks):
            self.in_up(k).wait_send()

        @pl.when(self.inner)
        def _():
            for k in range(self.blocks):
                self.out_down(k).wait_send()


def mode_sum_kernel(in_ref, out_ref, up_ref, down_ref, send_ref, sems):
    line = Line(lambda k: in_ref[k], out_ref, up_ref, down_ref, send_ref, sems)
    barrier = pltpu.get_barrier_semaphore()
    pl.semaphore_wait(barrier, line.greet(barrier))
    for t in range(line.steps()):
        line.step(t)
    line.drain()


def sum_over_mode(local):
    shape = local.shape
    blocked = local.reshape(BLOCKS, -1, shape[-1])
    buffer = pltpu.VMEM(blocked.shape, F32)
    return pl.pallas_call(
        mode_sum_kernel,
        out_shape=jax.ShapeDtypeStruct(blocked.shape, F32),
        in_specs=[VMEM_SPEC],
        out_specs=VMEM_SPEC,
        scratch_shapes=[buffer, buffer, buffer, pltpu.SemaphoreType.DMA((4, BLOCKS))],
        compiler_params=pltpu.CompilerParams(collective_id=0, has_side_effects=True, vmem_limit_bytes=60 << 20),
        name="mode_sum",
    )(blocked).reshape(shape)


def finish_kernel(grad_ref, rim_ref, probe_ref, out_ref, probe_out_ref,
                  up_ref, down_ref, send_ref, rim_in_ref, part_ref, got_ref, sems, rim_sems, probe_sems):
    tiles = lax.axis_size("tile")
    me = lax.axis_index("tile")
    bits = tiles.bit_length() - 1
    has_next, has_last = me < tiles - 1, me > 0

    def rim_copy(k):
        return pltpu.make_async_remote_copy(
            src_ref=rim_ref.at[k], dst_ref=rim_in_ref.at[k],
            send_sem=rim_sems.at[0, k], recv_sem=rim_sems.at[1, k],
            device_id={"tile": me + 1}, device_id_type=MESH)

    def own(k):
        return send_ref[k]

    line = Line(own, out_ref, up_ref, down_ref, send_ref, sems)

    def other(bit):
        low = lax.rem(me // (1 << bit), 2)
        return me + (1 - 2 * low) * (1 << bit)

    side = lax.rem(me, 2)

    def probe_copy(step, source, target):
        return pltpu.make_async_remote_copy(
            src_ref=source, dst_ref=target,
            send_sem=probe_sems.at[0, step], recv_sem=probe_sems.at[1, step],
            device_id={"tile": other((bits - step) % bits)}, device_id_type=MESH)

    def exchange(step):
        if step == 0:
            return probe_copy(0, probe_ref.at[1 - side], got_ref.at[0])
        if step < bits:
            return probe_copy(step, part_ref.at[step - 1], got_ref.at[step])
        return probe_copy(step, part_ref.at[bits - 1], probe_out_ref.at[side])

    barrier = pltpu.get_barrier_semaphore()
    count = line.greet(barrier)
    for bit in range(bits):
        pl.semaphore_signal(barrier, inc=1, device_id={"tile": other(bit)}, device_id_type=MESH)

    @pl.when(has_next)
    def _():
        pl.semaphore_signal(barrier, inc=1, device_id={"tile": me + 1}, device_id_type=MESH)

    @pl.when(has_last)
    def _():
        pl.semaphore_signal(barrier, inc=1, device_id={"tile": me - 1}, device_id_type=MESH)

    pl.semaphore_wait(barrier, count + bits + has_next.astype(jnp.int32) + has_last.astype(jnp.int32))

    exchange(0).start()

    @pl.when(has_next)
    def _():
        for k in range(line.blocks):
            rim_copy(k).start()

    for t in range(line.steps()):
        if t < line.blocks:
            @pl.when(has_last)
            def _():
                rim_copy(t).wait_recv()
                send_ref[t] = grad_ref[t] + rim_in_ref[t]

            @pl.when(jnp.logical_not(has_last))
            def _():
                send_ref[t] = grad_ref[t]
        line.step(t)
        bit = 0 if t == 1 else (t - 4) // 5
        if t == 1 or (t % 5 == 4 and 0 < bit < bits):
            exchange(bit).wait_recv()
            part_ref[bit] = (probe_ref[side] if bit == 0 else part_ref[bit - 1]) + got_ref[bit]
            exchange(bit + 1).start()
    probe_out_ref[side] = part_ref[bits - 1]
    exchange(bits).wait_recv()
    for step in range(bits + 1):
        exchange(step).wait_send()
    line.drain()

    @pl.when(has_next)
    def _():
        for k in range(line.blocks):
            rim_copy(k).wait_send()


def finish(grad, rim, grad_probe):
    bits = lax.axis_size("tile").bit_length() - 1
    blocked = (BLOCKS, -1, grad.shape[-1])
    own, edge = grad.reshape(blocked), rim.reshape(blocked)
    halves = grad_probe.reshape(2, -1, grad_probe.shape[-1])
    buffer = pltpu.VMEM(own.shape, F32)
    parts = pltpu.VMEM((bits, *halves.shape[1:]), F32)
    object_grad, probe_grad = pl.pallas_call(
        finish_kernel,
        out_shape=(jax.ShapeDtypeStruct(own.shape, F32), jax.ShapeDtypeStruct(halves.shape, F32)),
        in_specs=[VMEM_SPEC] * 3,
        out_specs=(VMEM_SPEC, VMEM_SPEC),
        scratch_shapes=[buffer, buffer, buffer, buffer, parts, parts,
                        pltpu.SemaphoreType.DMA((4, BLOCKS)), pltpu.SemaphoreType.DMA((2, BLOCKS)),
                        pltpu.SemaphoreType.DMA((2, bits + 1))],
        compiler_params=pltpu.CompilerParams(collective_id=1, has_side_effects=True, vmem_limit_bytes=60 << 20),
        name="finish",
    )(own, edge, halves)
    return object_grad.reshape(grad.shape), probe_grad.reshape(grad_probe.shape)


def per_device(object_field, probe, measured, prop_phase, counts, row_offset, col_offset):
    layers, _, tile_rows, columns = object_field.shape
    width = probe.shape[-1]
    local_modes = probe.shape[0]
    modes = local_modes * lax.axis_size("mode")
    slots = row_offset.shape[0]
    next_rows = shifted(object_field, "tile", -1)
    dft = jnp.asarray(dft_constants(width))
    spectral = jnp.concatenate([jnp.cos(prop_phase)[None], jnp.sin(prop_phase)[None], measured])
    spectral = to_even_odd(spectral)
    prop, measured = spectral[:2], spectral[2:]

    per_mode = pl.BlockSpec((1, 1, 2, width, width), lambda s, m, *_: (s, m, 0, 0, 0))
    per_slot = pl.BlockSpec((1, width, width), lambda s, m, *_: (s, 0, 0))
    ext_shape = pltpu.VMEM((layers, 2, tile_rows + width, columns), F32)
    window_shape = pltpu.VMEM((layers, 2, width, width), F32)
    table_shapes = [pltpu.VMEM((2, 2, width, 3 * width), BF16), pltpu.VMEM((2, 2, 3 * width, width), BF16)]
    per_window = pl.BlockSpec((1, layers, 2, width, width), lambda s, m, *_: (s, 0, 0, 0, 0))
    field = jax.ShapeDtypeStruct((slots, local_modes, 2, width, width), F32)
    params = pltpu.CompilerParams(dimension_semantics=("arbitrary", "arbitrary"), vmem_limit_bytes=60 << 20)

    before, far, local_power, windows = pl.pallas_call(
        forward_kernel,
        out_shape=(field, field, jax.ShapeDtypeStruct((slots, width, width), F32),
                   jax.ShapeDtypeStruct((slots, layers, 2, width, width), F32)),
        grid_spec=pltpu.PrefetchScalarGridSpec(
            num_scalar_prefetch=3,
            grid=(slots, local_modes),
            in_specs=[VMEM_SPEC] * 5,
            out_specs=(per_mode, per_mode, per_slot, per_window),
            scratch_shapes=[ext_shape, *table_shapes],
        ),
        compiler_params=params,
        name="forward",
    )(counts, row_offset, col_offset, object_field, next_rows, probe, prop, dft)

    power = sum_over_mode(local_power)

    whole = lambda shape: pl.BlockSpec(shape, lambda s, m, *_: (0,) * len(shape))
    grad, rim, grad_probe = pl.pallas_call(
        functools.partial(backward_kernel, modes=modes),
        out_shape=(
            jax.ShapeDtypeStruct(object_field.shape, F32),
            jax.ShapeDtypeStruct((layers, 2, width, columns), F32),
            jax.ShapeDtypeStruct(probe.shape, F32),
        ),
        grid_spec=pltpu.PrefetchScalarGridSpec(
            num_scalar_prefetch=3,
            grid=(slots, local_modes),
            in_specs=[VMEM_SPEC] * 3 + [per_mode, per_mode, per_slot, per_slot, per_window],
            out_specs=(whole(object_field.shape), whole((layers, 2, width, columns)), whole(probe.shape)),
            scratch_shapes=[window_shape, ext_shape, *table_shapes],
        ),
        compiler_params=params,
        name="backward",
    )(counts, row_offset, col_offset, probe, prop, dft, before, far, power, measured, windows)

    return finish(grad, rim, grad_probe)


def solution(mesh):
    placed = (
        P(None, None, "tile", None),
        P("mode", None, None, None),
        P("tile", None, None),
        P(),
        P("tile"),
        P("tile"),
        P("tile"),
    )
    return jax.shard_map(
        per_device,
        mesh=mesh,
        in_specs=placed,
        out_specs=(P(None, None, "tile", None), P("mode", None, None, None)),
        check_vma=False,
    )
```
